32 devices in a mesh: ctx: 8 (over z, y), fsdp: 4 (over x, core).
Axes of the slice: x: 2, y: 2, z: 4, core: 2. Of those that a mesh axis runs over, the one named last changes fastest.
Arguments:
- queries: bfloat16 [4, 3072, 1024], P('fsdp', 'ctx'), may hold values from -27 to 27
- keys: bfloat16 [4, 3072, 1024], P('fsdp', 'ctx'), may hold values from -27 to 27
- values: bfloat16 [4, 3072, 1024], P('fsdp', 'ctx'), may hold values from -6 to 6
- upstream: bfloat16 [4, 3072, 2048], P('fsdp', 'ctx'), may hold values from -6 to 6
- out_weight: bfloat16 [1024, 2048], P('fsdp'), may hold values from -0.1875 to 0.1875
- slopes: float32 [8], replicated, may hold values from 0.002 to 0.05
- patch_index: int32 [4, 3072], P('fsdp'), may hold values from 0 to 9213, as said below
- pair_lists: int32 [4, 2, 360], P('fsdp', None, 'ctx'), may hold values from 0 to 14, as said below
- pair_counts: int32 [4, 8], P('fsdp', 'ctx'), may hold values from 3 to 45, as said below
Outputs:
- grad_queries: bfloat16 [4, 3072, 1024], P('fsdp', 'ctx')
- grad_keys: bfloat16 [4, 3072, 1024], P('fsdp', 'ctx')
- grad_values: bfloat16 [4, 3072, 1024], P('fsdp', 'ctx')
- grad_out_weight: float32 [1024, 2048], P('fsdp', 'ctx')
The draws below stay inside these ranges and needn't reach their ends.
Inputs may be any that keep to these rules, and one draw needn't show every extreme that they name: `patch_index`: along each folio the numbers rise strictly, by 1 to 3 from one token to the next except before the last token, start at 0 and end at 9213. `pair_lists`: the first pair_counts entries of a device's list are distinct pairs (q, w) with q < 3 and w < 15, in no particular order; every device lists the 3 pairs (q, 6 + q). Entries from the count on are arbitrary pairs of the same ranges and are not attended. `pair_counts`: in every folio some device lists all 45 pairs.
All inputs are finite; a program needn't handle non-finite values.
Results may differ from the reference program's by a relative error of at most 0.015.
Values may be sent and summed in bfloat16 or wider, within the bound.
A program may use at most 192 MiB of HBM per device.

```python
import math
import jax
import jax.numpy as jnp
from jax import lax

D = 2048
HEADS = 8
HDIM = 128
HD = 1024
BLOCK = 128
REACH = 2
GRID = 1024
TOK_DEV = 384
QB = 3
WB = 15
MAXP = 45
SEQ = 3072
N_CTX = 8
N_FSDP = 4


def query_key_draw(key):
    shape = (N_FSDP, SEQ, HD)
    keys_raw = jax.random.truncated_normal(jax.random.fold_in(key, 101), -6.0, 6.0, shape, jnp.float32)
    queries_raw = jax.random.truncated_normal(jax.random.fold_in(key, 102), -6.0, 6.0, shape, jnp.float32)
    return (queries_raw, keys_raw)


def draw_queries(key, part):
    return query_key_draw(key)[0].astype(jnp.bfloat16)


def draw_keys(key, part):
    return query_key_draw(key)[1].astype(jnp.bfloat16)


def draw_patch_index(key, part):
    gaps = jax.random.randint(jax.random.fold_in(key, 201), (N_FSDP, SEQ), 1, 4)
    placed = jnp.cumsum(gaps, axis=1) - gaps[:, :1]
    position = jnp.arange(SEQ)[None, :]
    placed = jnp.where(position == SEQ - 1, 3 * (SEQ - 1), placed)
    return placed.astype(jnp.int32)


def pair_draw(key):
    levels = jax.random.randint(jax.random.fold_in(key, 301), (N_FSDP, N_CTX), 0, 8)
    full_device = jax.random.randint(jax.random.fold_in(key, 302), (N_FSDP,), 0, N_CTX)
    coins = jax.random.randint(jax.random.fold_in(key, 303), (N_FSDP, N_CTX, QB, WB), 0, 8)
    query_ids = jnp.arange(QB)[:, None]
    slot_ids = jnp.arange(WB)[None, :]
    diagonal = slot_ids == query_ids + REACH * QB
    devices = jnp.arange(N_CTX)
    chosen = diagonal[None, None] | (coins < levels[:, :, None, None]) | (devices[None, :, None, None] == full_device[:, None, None, None])
    chosen = chosen.reshape(N_FSDP, N_CTX, MAXP).astype(jnp.int32)
    noise = jax.random.randint(jax.random.fold_in(key, 304), (N_FSDP, N_CTX, MAXP), 0, 2 ** 20)
    order_key = (1 - chosen) * 2 ** 30 + noise * MAXP + jnp.arange(MAXP)[None, None, :]
    ranking = jnp.argsort(order_key, axis=2)
    pair_query = ranking // WB
    pair_slot = ranking % WB
    stacked = jnp.stack([pair_query, pair_slot], axis=1)
    pair_rows = stacked.reshape(N_FSDP, 2, N_CTX * MAXP)
    counts = jnp.sum(chosen, axis=2)
    return (pair_rows.astype(jnp.int32), counts.astype(jnp.int32))


def draw_pair_lists(key, part):
    return pair_draw(key)[0]


def draw_pair_counts(key, part):
    return pair_draw(key)[1]


def spiked(values, stream_key, source, target, blocks, factor):
    def block_of(axis_at):
        return (jnp.arange(values.shape[axis_at]) // (values.shape[axis_at] // blocks)).reshape((-1,) + (1,) * (values.ndim - 1 - axis_at))

    near = jax.random.permutation(stream_key, blocks)[block_of(target)]
    other_side = (block_of(target) + blocks // 2) % blocks
    return jnp.where((block_of(source) == near) | (block_of(source) == other_side), factor * values, values)


def block_scale(key, dims, pieces, least, high):
    gain = 1.0
    for axis_at, parts in pieces:
        draws = jax.random.uniform(jax.random.fold_in(jax.random.fold_in(key, 6), axis_at), (parts,), jnp.float32, least / len(pieces), high / len(pieces))
        gain = gain * jnp.repeat(jnp.exp(draws), dims[axis_at] // parts).reshape((-1,) + (1,) * (len(dims) - 1 - axis_at))
    return gain


def normal_values(rng, extent, width, limit, split=(), kind=jnp.bfloat16):
    factor_of = block_scale(rng, extent, split, -0.22, 0.18) if split else 1.0
    entries = jax.random.normal(rng, extent, jnp.float32) * width * factor_of
    return jnp.minimum(jnp.maximum(entries, -limit), limit).astype(kind)


def bell_draw_with(key, extent, scale, most, shards, heavy, kind=jnp.bfloat16):
    entries = scale * jax.random.normal(key, extent, jnp.float32)
    if shards:
        entries = entries * block_scale(key, extent, shards, -0.22, 0.18)
    return jnp.clip(spiked(entries, jax.random.fold_in(key, 3), *heavy), -most, most).astype(kind)


def setup_inputs(seed: int = 0) -> dict:
    streams_of = jax.random.split(jax.random.key(seed), 10)
    queries = draw_queries(jax.random.fold_in(streams_of[9], 71), 0)
    keys = draw_keys(jax.random.fold_in(streams_of[9], 71), 0)
    values = normal_values(streams_of[2], (N_FSDP, SEQ, HD), 1.0, 6.0, ((0, 4), (1, 8)))
    upstream = bell_draw_with(streams_of[3], (N_FSDP, SEQ, D), 1.0, 6.0, ((0, 4), (1, 8)), (1, 2, 8, 2.0))
    out_weight = normal_values(streams_of[4], (HD, D), HD ** -0.5, 0.1875, ((0, 4),))
    slopes = jnp.clip(jnp.exp(jax.random.uniform(streams_of[5], (HEADS,), jnp.float32, math.log(0.002), math.log(0.05))), 0.002, 0.05)
    patch_index = draw_patch_index(jax.random.fold_in(streams_of[9], 71), 0)
    pair_lists = draw_pair_lists(jax.random.fold_in(streams_of[9], 71), 0)
    pair_counts = draw_pair_counts(jax.random.fold_in(streams_of[9], 71), 0)
    return dict(queries=queries, keys=keys, values=values, upstream=upstream, out_weight=out_weight, slopes=slopes, patch_index=patch_index, pair_lists=pair_lists, pair_counts=pair_counts)


masked_fill = -1e+30

def reference(queries, keys, values, upstream, out_weight, slopes, patch_index, pair_lists, pair_counts):
    scaling = 1.0 / math.sqrt(HDIM)
    out_grad_all = lax.optimization_barrier(jnp.dot(upstream.reshape(N_FSDP * SEQ, D), out_weight.T, preferred_element_type=jnp.float32).astype(jnp.bfloat16)).reshape(N_FSDP, SEQ, HD)
    offsets = jnp.arange(-REACH, REACH + 1, dtype=jnp.int32)
    inside = jnp.arange(TOK_DEV, dtype=jnp.int32)
    pair_ids = jnp.arange(MAXP, dtype=jnp.int32)
    query_ids = jnp.arange(QB, dtype=jnp.int32)
    slot_ids = jnp.arange(WB, dtype=jnp.int32)

    def device_step(running, flat_index):
        key_sums, value_sums = running
        folio_index = (flat_index // N_CTX).astype(jnp.int32)
        device = (flat_index % N_CTX).astype(jnp.int32)
        own_rows = device * TOK_DEV + inside
        owners = (device + offsets) % N_CTX
        window_rows = (owners[:, None] * TOK_DEV + inside[None, :]).reshape(WB * BLOCK)
        query_heads = queries[folio_index][own_rows].astype(jnp.float32).reshape(TOK_DEV, HEADS, HDIM)
        key_heads = keys[folio_index][window_rows].astype(jnp.float32).reshape(WB * BLOCK, HEADS, HDIM)
        value_heads = values[folio_index][window_rows].astype(jnp.float32).reshape(WB * BLOCK, HEADS, HDIM)
        out_grad = out_grad_all[folio_index][own_rows].astype(jnp.float32).reshape(TOK_DEV, HEADS, HDIM)
        positions = patch_index[folio_index]
        query_pos = positions[own_rows]
        key_pos = positions[window_rows]
        distance = (jnp.abs(query_pos[:, None] // GRID - key_pos[None, :] // GRID) + jnp.abs(query_pos[:, None] % GRID - key_pos[None, :] % GRID)).astype(jnp.float32)
        pair_rows = lax.dynamic_slice(pair_lists, (folio_index, jnp.zeros((), jnp.int32), device * MAXP), (1, 2, MAXP))[0]
        listed = pair_ids < pair_counts[folio_index, device]
        block_mask = jnp.any(listed[:, None, None] & (pair_rows[0][:, None, None] == query_ids[None, :, None]) & (pair_rows[1][:, None, None] == slot_ids[None, None, :]), axis=0)
        token_mask = jnp.broadcast_to(block_mask[:, None, :, None], (QB, BLOCK, WB, BLOCK)).reshape(TOK_DEV, WB * BLOCK)
        logits = jnp.einsum('qhd,khd->hqk', query_heads, key_heads) * scaling - slopes[:, None, None] * distance[None]
        logits = jnp.where(token_mask[None], logits, masked_fill)
        row_top = lax.optimization_barrier(jnp.max(logits, axis=2))
        exp_terms = jnp.where(token_mask[None], jnp.exp(logits - row_top[:, :, None]), 0.0)
        row_total = lax.optimization_barrier(jnp.sum(exp_terms, axis=2))
        exp_rounded = lax.optimization_barrier(exp_terms.astype(jnp.bfloat16)).astype(jnp.float32)
        attended = (jnp.einsum('hqk,khd->qhd', exp_rounded, value_heads) / row_total.T[:, :, None]).astype(jnp.bfloat16)
        attended_wide = lax.optimization_barrier(attended).astype(jnp.float32)
        row_delta = lax.optimization_barrier(jnp.sum(out_grad * attended_wide, axis=2)).T
        prob_values = exp_terms / row_total[:, :, None]
        prob_grad = jnp.einsum('qhd,khd->hqk', out_grad, value_heads)
        score_grad = lax.optimization_barrier((prob_values * (prob_grad - row_delta[:, :, None])).astype(jnp.bfloat16)).astype(jnp.float32)
        query_grad = (jnp.einsum('hqk,khd->qhd', score_grad, key_heads) * scaling).astype(jnp.bfloat16)
        key_part = lax.optimization_barrier((jnp.einsum('hqk,qhd->khd', score_grad, query_heads) * scaling).astype(jnp.bfloat16)).astype(jnp.float32)
        prob_rounded = lax.optimization_barrier(prob_values.astype(jnp.bfloat16)).astype(jnp.float32)
        value_part = lax.optimization_barrier(jnp.einsum('hqk,qhd->khd', prob_rounded, out_grad).astype(jnp.bfloat16)).astype(jnp.float32)
        key_sums = key_sums.at[folio_index, window_rows].add(key_part.reshape(WB * BLOCK, HD))
        value_sums = value_sums.at[folio_index, window_rows].add(value_part.reshape(WB * BLOCK, HD))
        return ((key_sums, value_sums), (attended.reshape(TOK_DEV, HD), query_grad.reshape(TOK_DEV, HD)))
    start_sums = (jnp.zeros((N_FSDP, SEQ, HD), jnp.float32), jnp.zeros((N_FSDP, SEQ, HD), jnp.float32))
    (key_sums, value_sums), (attended_all, query_all) = lax.scan(device_step, start_sums, jnp.arange(N_FSDP * N_CTX, dtype=jnp.int32))
    attended_all = attended_all.reshape(N_FSDP * SEQ, HD)
    grad_queries = query_all.reshape(N_FSDP, SEQ, HD)
    weight_grad = jnp.dot(attended_all.T, upstream.reshape(N_FSDP * SEQ, D), preferred_element_type=jnp.float32) / math.sqrt(N_FSDP * SEQ)
    return (grad_queries, key_sums.astype(jnp.bfloat16), value_sums.astype(jnp.bfloat16), weight_grad)
```

```python
import functools
import math

import jax
import jax.numpy as jnp
from jax import lax
from jax.experimental import pallas as pl
from jax.experimental.pallas import tpu as pltpu
from jax.sharding import PartitionSpec as P

BLOCK = 128
REACH = 2
GRID = 1024
GRID_BITS = 10
FAR = 1e32
MESH = pl.DeviceIdType.MESH
F32 = jnp.float32
BF16 = jnp.bfloat16


def nt(a, b):
    return lax.dot_general(a, b, (((1,), (1,)), ((), ())), preferred_element_type=F32)


def nn(a, b):
    return lax.dot_general(a, b, (((1,), (0,)), ((), ())), preferred_element_type=F32)


def tn(a, b):
    return lax.dot_general(a, b, (((0,), (0,)), ((), ())), preferred_element_type=F32)


def greet(targets):
    barrier = pltpu.get_barrier_semaphore()
    for target in targets:
        pl.semaphore_signal(barrier, inc=1, device_id=target, device_id_type=MESH)
    pl.semaphore_wait(barrier, len(targets))


def remote(src, dst, send_sem, recv_sem, target):
    return pltpu.make_async_remote_copy(
        src_ref=src, dst_ref=dst, send_sem=send_sem, recv_sem=recv_sem, device_id=target, device_id_type=MESH
    )


def head_span(h, size):
    return pl.ds(pl.multiple_of(h * size, size), size)


def build_distance(far, edge, col_ref, pos_ref, mask_ref, key_row, query_row, mask_at, slot, a, tokens):
    at = pl.multiple_of(query_row * tokens, BLOCK)
    query = pos_ref[0:1, pl.ds(at, tokens)]
    qr = jnp.right_shift(query, GRID_BITS).astype(F32)
    qg = jnp.bitwise_and(query, GRID - 1).astype(F32)
    for b in range(tokens // BLOCK):
        rows = pl.ds(pl.multiple_of(key_row * tokens + b * BLOCK, BLOCK), BLOCK)
        kr = col_ref[0, rows, :]
        kg = col_ref[1, rows, :]
        mask = mask_ref[slot, a, pl.ds(mask_at + b, 1), :]
        for q in range(tokens // BLOCK):
            lanes = slice(q * BLOCK, (q + 1) * BLOCK)
            dist = jnp.abs(kr - qr[:, lanes]) + jnp.abs(kg - qg[:, lanes])
            far[edge, b * BLOCK : (b + 1) * BLOCK, lanes] = jnp.where(mask[:, lanes] > 0.5, dist, FAR)


def fused_kernel(
    heads,
    weight_scale,
    slopes_ref,
    q_ref,
    k_ref,
    v_ref,
    up_ref,
    w_ref,
    pos_ref,
    pairs_ref,
    count_ref,
    dq_ref,
    dk_ref,
    dv_ref,
    wg_ref,
    kb_ref,
    vb_ref,
    qb_ref,
    gb_ref,
    og_ref,
    att_ref,
    attc_ref,
    dqs_ref,
    dks_ref,
    dvs_ref,
    cm_ref,
    mask_ref,
    stats_ref,
    col_ref,
    wbuf_ref,
    far_ref,
    fark_ref,
    top_ref,
    total_ref,
    acc_ref,
    dka_ref,
    dva_ref,
    part_ref,
    pland_ref,
    wsum_ref,
    ysum_ref,
    zland_ref,
    zs_sem,
    zr_sem,
    ts_sem,
    tr_sem,
    ys_sem,
    yr_sem,
    wsend_sem,
    wrecv_sem,
    gsend_sem,
    grecv_sem,
    ysem,
    zsend_sem,
    zrecv_sem,
):
    tokens, width = q_ref.shape
    size = width // heads
    hl = heads // 2
    hw = width // 2
    blocks = tokens // BLOCK
    scaling = 1.0 / math.sqrt(size)
    n = lax.axis_size("ctx")
    nf = lax.axis_size("fsdp")
    me = lax.axis_index("ctx")
    fs = lax.axis_index("fsdp")
    wrows = w_ref.shape[0]
    model = up_ref.shape[1]
    half = n // 2
    wide = wsum_ref.shape[3]
    mask_rows = mask_ref.shape[2]
    y = lax.rem(me, 2)
    ny = 1 - y
    chunk = lax.div(me, 2)
    partner = {"ctx": me + 1 - 2 * y}
    ways = ({"ctx": lax.rem(me + 2, n)}, {"ctx": lax.rem(me + n - 2, n)})
    twin = fs + 1 - 2 * lax.rem(fs, 2)
    facing = lax.rem(fs + 2, nf)
    corner = lax.rem(twin + 2, nf)
    across = [{"ctx": lax.rem(me + 2 * d, n)} for d in range(1, half)]
    own_rows = pl.ds(pl.multiple_of(y * tokens, BLOCK), tokens)
    other_rows = pl.ds(pl.multiple_of(ny * tokens, BLOCK), tokens)
    own_cols = pl.ds(pl.multiple_of(y * hw, BLOCK), hw)
    other_cols = pl.ds(pl.multiple_of(ny * hw, BLOCK), hw)

    def rows_of(a):
        return pl.ds(pl.multiple_of(a * tokens, BLOCK), tokens)

    def chunk_of(slot):
        return lax.rem(chunk + lax.rem(slot + 1, 3) - 1 + half, half)

    greet([partner] + across + [{"fsdp": twin}, {"fsdp": facing}])

    own_src = (k_ref, v_ref, q_ref, og_ref)
    chunk_buf = (kb_ref, vb_ref, qb_ref, gb_ref)

    def along(piece, part, way):
        which = min(piece, 3)
        buf = chunk_buf[which]
        rows = (own_rows, other_rows)[part]
        if piece < 3:
            cols, own = pl.ds(0, hw), own_cols
        else:
            h = piece - 3
            cols = pl.ds(h * size, size)
            own = pl.ds(pl.multiple_of(y * hw + h * size, BLOCK), size)
        src = own_src[which].at[:, own] if part == 0 else buf.at[0, rows, cols]
        return remote(src, buf.at[2 - way, rows, cols], zs_sem.at[piece, part, way], zr_sem.at[piece, part, way], ways[way])

    def start_along(piece, part):
        for way in (0, 1):
            along(piece, part, way).start()

    def landed(piece, part):
        for way in (0, 1):
            along(piece, part, way).wait_recv()

    def small(kind, way):
        ref = (stats_ref, cm_ref)[kind]
        return remote(ref.at[0], ref.at[2 - way], ts_sem.at[kind, way], tr_sem.at[kind, way], ways[way])

    def over(piece, mine=True):
        if piece < 4:
            src = own_src[piece].at[:, other_cols]
            dst = chunk_buf[piece].at[0, own_rows if mine else other_rows, :]
        elif piece == 4:
            src = cm_ref.at[0, y]
            dst = cm_ref.at[0, y if mine else ny]
        elif piece == 5:
            src = attc_ref.at[other_rows, :]
            dst = att_ref.at[:, own_cols if mine else other_cols]
        elif piece == 6:
            src = dqs_ref
            dst = dq_ref.at[:, own_cols if mine else other_cols]
        else:
            h = (piece - 7) // 2
            stage, out = ((dks_ref, dk_ref), (dvs_ref, dv_ref))[(piece - 7) % 2]
            src = stage.at[:, pl.ds(h * size, size)]
            at = (y if mine else ny) * hw + h * size
            dst = out.at[:, pl.ds(pl.multiple_of(at, BLOCK), size)]
        return remote(src, dst, ys_sem.at[piece], yr_sem.at[piece], partner)

    def met(piece):
        over(piece, False).wait_recv()

    for piece in (0, 1):
        over(piece).start()
        start_along(piece, 0)
    wcopies = [
        remote(
            wbuf_ref.at[1] if d == 2 else w_ref,
            wbuf_ref.at[d],
            wsend_sem.at[d],
            wrecv_sem.at[d],
            {"fsdp": facing if d == 1 else twin},
        )
        for d in range(3)
    ]
    wcopies[1].start()
    wcopies[0].start()
    over(2).start()

    lane = lax.broadcasted_iota(jnp.int32, (1, pairs_ref.shape[1]), 1)
    listed = lane < count_ref[0:1, 0:1]
    slot_iota = lax.broadcasted_iota(jnp.int32, (mask_rows, pairs_ref.shape[1]), 0)
    lane_iota = lax.broadcasted_iota(jnp.int32, (mask_rows, BLOCK), 1)
    compact = jnp.zeros((mask_rows, BLOCK), F32)
    for q in range(blocks):
        picked = jnp.where(listed & (pairs_ref[0:1, :] == q), pairs_ref[1:2, :], -1)
        hit = jnp.where(slot_iota == picked, 1.0, 0.0).astype(F32)
        hit = jnp.max(hit, axis=1, keepdims=True)
        compact = jnp.where(lane_iota == q, hit, compact)
    cm_ref[0, y] = compact
    over(4).start()

    def expand(slot, a):
        small_mask = cm_ref[slot, a]
        for q in range(blocks):
            mask_ref[slot, a, :, q * BLOCK : (q + 1) * BLOCK] = jnp.broadcast_to(
                small_mask[:, q : q + 1], (mask_rows, BLOCK)
            )

    expand(0, y)

    @pl.loop(0, 6)
    def _(i):
        slot = lax.div(i, 2)
        node = 2 * chunk_of(slot) + lax.rem(i, 2)
        place = pos_ref[0:1, rows_of(node)]
        for c, part in enumerate((jnp.right_shift(place, GRID_BITS), jnp.bitwise_and(place, GRID - 1))):
            wide_part = jnp.broadcast_to(part.astype(F32), (BLOCK, tokens))
            col_ref[c, rows_of(i), :] = wide_part.T

    kb_ref[0, own_rows, :] = k_ref[:, own_cols]
    vb_ref[0, own_rows, :] = v_ref[:, own_cols]
    qb_ref[0, own_rows, :] = q_ref[:, own_cols]
    top_ref[...] = jnp.full(top_ref.shape, -1e30, F32)
    total_ref[...] = jnp.zeros(total_ref.shape, F32)
    acc_ref[...] = jnp.zeros(acc_ref.shape, F32)
    dka_ref[...] = jnp.zeros(dka_ref.shape, F32)
    dva_ref[...] = jnp.zeros(dva_ref.shape, F32)

    def measure(far, edge, qs, a, ks, b):
        shift = 2 * ((lax.rem(ks + 1, 3) - 1) - (lax.rem(qs + 1, 3) - 1)) + b - a
        build_distance(
            far, edge, col_ref, pos_ref, mask_ref, 2 * ks + b, 2 * chunk_of(qs) + a,
            (shift + REACH) * blocks, qs, a, tokens,
        )

    def local_edge(e):
        if isinstance(e, int) and e == 0:
            return y, 0, y
        c2 = lax.div(e - 1, 2)
        c1 = e - 1 - 2 * c2
        return ny + c2 * (y - ny), 0, ny + c1 * (y - ny)

    def far_edge(e):
        phase = lax.div(e - 4, 3)
        j = e - 4 - 3 * phase
        t = y + phase * (ny - y)
        c2 = lax.div(j, 2)
        c1 = j - 2 * c2
        c0 = 1 - c1 - c2
        return c0 + c2 * t, c0 + 2 * c1 + c2 * (1 + t), t

    def look(e, edge):
        a, ks, b = edge
        measure(far_ref, e, 0, a, ks, b)
        ka, qa = rows_of(b), rows_of(a)

        @pl.loop(0, hl)
        def _(h):
            hs = head_span(h, size)
            i = a * hl + h
            s = nt(kb_ref[ks, ka, hs], qb_ref[0, qa, hs]) * scaling - slopes_ref[y * hl + h] * far_ref[e]
            old = top_ref[i]
            new = jnp.maximum(old, jnp.max(s, axis=0, keepdims=True))
            factor = jnp.exp(old - new)
            p = jnp.exp(s - new)
            top_ref[i] = new
            total_ref[i] = total_ref[i] * factor + jnp.sum(p, axis=0, keepdims=True)
            acc_ref[i] = acc_ref[i] * factor + tn(vb_ref[ks, ka, hs], p.astype(BF16))

    def project(block, owner):
        cols = pl.ds(pl.multiple_of(owner * wrows, BLOCK), wrows)
        og_ref[:, cols] = nt(up_ref[...], block[...]).astype(BF16)

    look(0, local_edge(0))
    project(w_ref, fs)
    for piece in (0, 1):
        met(piece)
        start_along(piece, 1)
    start_along(2, 0)
    met(4)
    expand(0, ny)
    met(2)
    start_along(2, 1)

    @pl.loop(1, 4)
    def _(e):
        look(e, local_edge(e))

    wcopies[1].wait()
    wcopies[2].start()
    project(wbuf_ref.at[1], facing)
    wcopies[0].wait()
    project(wbuf_ref.at[0], twin)
    wcopies[2].wait()
    project(wbuf_ref.at[2], corner)
    over(3).start()
    gb_ref[0, own_rows, :] = og_ref[:, own_cols]

    for phase in (0, 1):
        landed(0, phase)
        landed(1, phase)

        @pl.loop(4 + 3 * phase, 7 + 3 * phase)
        def _(e):
            look(e, far_edge(e))

    met(3)

    @pl.loop(0, 2 * hl)
    def _(i):
        a = lax.div(i, hl)
        h = i - a * hl
        hs = head_span(h, size)
        rows = rows_of(a)
        total = total_ref[i]
        att = (acc_ref[i] / total).T.astype(BF16)
        attc_ref[rows, hs] = att
        stats_ref[0, pl.ds(a * 2 * hl + h, 1), :] = top_ref[i] + jnp.log(total)
        prod = gb_ref[0, rows, hs].astype(F32) * att.astype(F32)
        stats_ref[0, pl.ds(a * 2 * hl + hl + h, 1), :] = jnp.sum(prod.T, axis=0, keepdims=True)
        acc_ref[i] = jnp.zeros((size, tokens), F32)

    for kind in (0, 1):
        for way in (0, 1):
            small(kind, way).start()
    over(5).start()
    for h in range(hl):
        for part in (0, 1):
            start_along(3 + h, part)
    att_ref[:, own_cols] = attc_ref[own_rows, :]

    def part_of(owner):
        cols = pl.ds(pl.multiple_of(owner * wrows, BLOCK), wrows)
        return tn(att_ref[:, cols], up_ref[...])

    gcopies = [
        remote(
            part_ref.at[d],
            pland_ref.at[d],
            gsend_sem.at[d],
            grecv_sem.at[d],
            {"fsdp": facing if d == 2 else twin},
        )
        for d in range(3)
    ]

    def visit(far, e, qs, a, ks, b, h, to_query, to_key):
        hs = head_span(h, size)
        ka, qa = rows_of(b), rows_of(a)
        k, q, g = kb_ref[ks, ka, hs], qb_ref[qs, qa, hs], gb_ref[qs, qa, hs]
        s = nt(k, q) * scaling - slopes_ref[y * hl + h] * far[e]
        p = jnp.exp(s - stats_ref[qs, pl.ds(a * 2 * hl + h, 1), :])
        delta = stats_ref[qs, pl.ds(a * 2 * hl + hl + h, 1), :]
        ds = (p * (nt(vb_ref[ks, ka, hs], g) - delta)).astype(BF16)
        if to_query:
            i = a * hl + h
            acc_ref[i] = acc_ref[i] + tn(k, ds)
        if to_key:
            i = b * hl + h
            dka_ref[i] = dka_ref[i] + nn(ds, q)
            dva_ref[i] = dva_ref[i] + nn(p.astype(BF16), g)

    @pl.loop(0, 4)
    def _(e):
        first = 1 - lax.div(e + 3, 4)
        a, ks, b = local_edge(e + first)
        a = a + first * (y - ny)
        b = b + first * (y - ny)

        @pl.loop(0, hl)
        def _(h):
            visit(far_ref, e, 0, a, ks, b, h, True, True)

    met(5)
    part_ref[1] = part_of(corner).astype(BF16)
    gcopies[1].start()
    part_ref[0] = part_of(twin).astype(BF16)
    gcopies[0].start()

    def query_edges(first, last):
        @pl.loop(first, last)
        def _(e):
            a, ks, b = far_edge(e)

            @pl.loop(0, hl)
            def _(h):
                visit(far_ref, e, 0, a, ks, b, h, True, False)

    query_edges(4, 7)
    gcopies[1].wait()
    part_ref[2] = (part_of(facing) + pland_ref[1].astype(F32)).astype(BF16)
    gcopies[2].start()
    query_edges(7, 10)

    @pl.loop(0, hl)
    def _(h):
        hs = head_span(h, size)
        dqs_ref[:, hs] = (acc_ref[ny * hl + h].T * scaling).astype(BF16)
        dq_ref[:, pl.ds(pl.multiple_of(y * hw + h * size, BLOCK), size)] = (
            acc_ref[y * hl + h].T * scaling
        ).astype(BF16)

    over(6).start()

    for kind in (0, 1):
        for way in (0, 1):
            small(kind, way).wait_recv()
    for slot in (1, 2):
        for a in (0, 1):
            expand(slot, a)

    def key_edge(e):
        before = lax.div(e, 3)
        i = e - 3 * before
        p = lax.div(i, 2)
        r = lax.div(i + 1, 2)
        return 1 + before, p + before * (r - p), 0, r + before * (p - r)

    @pl.loop(0, 6)
    def _(e):
        measure(fark_ref, e, *key_edge(e))

    for part in (0, 1):
        landed(2, part)

    def to_key(h):
        for part in (0, 1):
            landed(3 + h, part)

        @pl.loop(0, 6)
        def _(e):
            visit(fark_ref, e, *key_edge(e), h, False, True)

        hs = pl.ds(h * size, size)
        out = pl.ds(pl.multiple_of(y * hw + h * size, BLOCK), size)
        dks_ref[:, hs] = (dka_ref[ny * hl + h] * scaling).astype(BF16)
        dvs_ref[:, hs] = dva_ref[ny * hl + h].astype(BF16)
        over(7 + 2 * h).start()
        over(8 + 2 * h).start()
        dk_ref[:, out] = (dka_ref[y * hl + h] * scaling).astype(BF16)
        dv_ref[:, out] = dva_ref[y * hl + h].astype(BF16)

    to_key(0)
    gcopies[0].wait()
    gcopies[2].wait()
    mine = part_of(fs) + pland_ref[0].astype(F32) + pland_ref[2].astype(F32)
    for c in range(n):
        at = c * (model // n) // wide * wide
        wsum_ref[c % 2, c // 2] = mine[:, at : at + wide].astype(BF16)
    ycopy = remote(wsum_ref.at[ny], ysum_ref, ysem.at[0], ysem.at[1], partner)
    ycopy.start()
    to_key(1)

    ycopy.wait()
    zcopies = []
    for d in range(half):
        k = lax.rem(chunk + d, half)
        pair_sum = wsum_ref[y, k].astype(F32) + ysum_ref[k].astype(F32)
        if d == 0:
            wg_ref[...] = pair_sum
            continue
        zland_ref[0, d - 1] = pair_sum.astype(BF16)
        copy = remote(
            zland_ref.at[0, d - 1], zland_ref.at[1, d - 1], zsend_sem.at[d - 1], zrecv_sem.at[d - 1], across[d - 1]
        )
        copy.start()
        zcopies.append(copy)

    for h in range(2, hl):
        to_key(h)

    total = wg_ref[...]
    for d in range(1, half):
        zcopies[d - 1].wait()
        total = total + zland_ref[1, d - 1].astype(F32)
    wg_ref[...] = total * weight_scale
    for piece in range(6, 7 + 2 * hl):
        met(piece)
    for piece in range(7 + 2 * hl):
        over(piece).wait_send()
    for piece in range(3 + hl):
        for part in (0, 1):
            for way in (0, 1):
                along(piece, part, way).wait_send()
    for kind in (0, 1):
        for way in (0, 1):
            small(kind, way).wait_send()


def on_device(
    queries, keys, values, upstream, out_weight, slopes, patch_index, pair_lists, pair_counts
):
    n = lax.axis_size("ctx")
    nf = lax.axis_size("fsdp")
    me = lax.axis_index("ctx")
    tokens, width = queries.shape[1:]
    model = upstream.shape[2]
    heads = slopes.shape[0]
    size = width // heads
    blocks = tokens // BLOCK
    window = 2 * REACH + 1
    slots = window * blocks
    mask_rows = -(-slots // 8) * 8

    vmem = pl.BlockSpec(memory_space=pltpu.VMEM)
    smem = pl.BlockSpec(memory_space=pltpu.SMEM)
    block = jax.ShapeDtypeStruct((tokens, width), BF16)
    pair_flops = 2 * tokens * tokens * window * width
    wrows = out_weight.shape[0]
    cut = model // n
    wide = max(cut, BLOCK)
    half = n // 2
    hl = heads // 2
    hw = width // 2
    chunks = pltpu.VMEM((3, 2 * tokens, hw), BF16)
    stage = pltpu.VMEM((tokens, hw), BF16)
    dq, dk, dv, weight_grad = pl.pallas_call(
        functools.partial(fused_kernel, heads, 1.0 / math.sqrt(tokens * n * nf)),
        out_shape=(block, block, block, jax.ShapeDtypeStruct((wrows, wide), F32)),
        in_specs=[smem] + [vmem] * 8,
        out_specs=(vmem,) * 4,
        scratch_shapes=[
            chunks,
            chunks,
            chunks,
            chunks,
            pltpu.VMEM((tokens, width), BF16),
            pltpu.VMEM((tokens, width), BF16),
            pltpu.VMEM((2 * tokens, hw), BF16),
            stage,
            stage,
            stage,
            pltpu.VMEM((3, 2, mask_rows, BLOCK), F32),
            pltpu.VMEM((3, 2, mask_rows, tokens), F32),
            pltpu.VMEM((3, 4 * hl, tokens), F32),
            pltpu.VMEM((2, 6 * tokens, BLOCK), F32),
            pltpu.VMEM((3,) + out_weight.shape, BF16),
            pltpu.VMEM((10, tokens, tokens), F32),
            pltpu.VMEM((6, tokens, tokens), F32),
            pltpu.VMEM((2 * hl, 1, tokens), F32),
            pltpu.VMEM((2 * hl, 1, tokens), F32),
            pltpu.VMEM((2 * hl, size, tokens), F32),
            pltpu.VMEM((2 * hl, tokens, size), F32),
            pltpu.VMEM((2 * hl, tokens, size), F32),
            pltpu.VMEM((3, wrows, model), BF16),
            pltpu.VMEM((3, wrows, model), BF16),
            pltpu.VMEM((2, half, wrows, wide), BF16),
            pltpu.VMEM((half, wrows, wide), BF16),
            pltpu.VMEM((2, half - 1, wrows, wide), BF16),
            pltpu.SemaphoreType.DMA((3 + hl, 2, 2)),
            pltpu.SemaphoreType.DMA((3 + hl, 2, 2)),
            pltpu.SemaphoreType.DMA((2, 2)),
            pltpu.SemaphoreType.DMA((2, 2)),
            pltpu.SemaphoreType.DMA((7 + 2 * hl,)),
            pltpu.SemaphoreType.DMA((7 + 2 * hl,)),
            pltpu.SemaphoreType.DMA((3,)),
            pltpu.SemaphoreType.DMA((3,)),
            pltpu.SemaphoreType.DMA((3,)),
            pltpu.SemaphoreType.DMA((3,)),
            pltpu.SemaphoreType.DMA((2,)),
            pltpu.SemaphoreType.DMA((half - 1,)),
            pltpu.SemaphoreType.DMA((half - 1,)),
        ],
        compiler_params=pltpu.CompilerParams(
            collective_id=0, has_side_effects=True, vmem_limit_bytes=58 * 2**20
        ),
        cost_estimate=pl.CostEstimate(
            flops=10 * pair_flops, bytes_accessed=400 * 2**20, transcendentals=0
        ),
        name="fused",
    )(slopes, queries[0], keys[0], values[0], upstream[0], out_weight, patch_index, pair_lists[0], pair_counts)
    if wide > cut:
        weight_grad = lax.dynamic_slice_in_dim(weight_grad, me * cut % wide, cut, 1)
    return (dq[None], dk[None], dv[None], weight_grad)


def solution(mesh):
    in_specs = (
        P("fsdp", "ctx", None),
        P("fsdp", "ctx", None),
        P("fsdp", "ctx", None),
        P("fsdp", "ctx", None),
        P("fsdp", None),
        P(),
        P("fsdp", None),
        P("fsdp", None, "ctx"),
        P("fsdp", "ctx"),
    )
    out_specs = (
        P("fsdp", "ctx", None),
        P("fsdp", "ctx", None),
        P("fsdp", "ctx", None),
        P("fsdp", "ctx"),
    )
    return jax.shard_map(
        on_device, mesh=mesh, in_specs=in_specs, out_specs=out_specs, check_vma=False
    )
```

```python
import functools
import math

import jax
import jax.numpy as jnp
from jax import lax
from jax.experimental import pallas as pl
from jax.experimental.pallas import tpu as pltpu
from jax.sharding import PartitionSpec as P

BLOCK = 128
REACH = 2
GRID = 1024
GRID_BITS = 10
SPLIT = 1
FAR = 1e32
MESH = pl.DeviceIdType.MESH
F32 = jnp.float32
BF16 = jnp.bfloat16


def nt(a, b):
    return lax.dot_general(a, b, (((1,), (1,)), ((), ())), preferred_element_type=F32)


def nn(a, b):
    return lax.dot_general(a, b, (((1,), (0,)), ((), ())), preferred_element_type=F32)


def tn(a, b):
    return lax.dot_general(a, b, (((0,), (0,)), ((), ())), preferred_element_type=F32)


def remote(src, dst, send_sem, recv_sem, target):
    return pltpu.make_async_remote_copy(
        src_ref=src, dst_ref=dst, send_sem=send_sem, recv_sem=recv_sem, device_id=target, device_id_type=MESH
    )


def head_span(h, size):
    return pl.ds(pl.multiple_of(h * size, size), size)


def build_distance(far, edge, col_ref, pos_ref, mask_ref, key_row, query_row, mask_at, slot, a, tokens):
    at = pl.multiple_of(query_row * tokens, BLOCK)
    query = pos_ref[0:1, pl.ds(at, tokens)]
    qr = jnp.right_shift(query, GRID_BITS).astype(F32)
    qg = jnp.bitwise_and(query, GRID - 1).astype(F32)
    for b in range(tokens // BLOCK):
        rows = pl.ds(pl.multiple_of(key_row * tokens + b * BLOCK, BLOCK), BLOCK)
        kr = col_ref[0, rows, :]
        kg = col_ref[1, rows, :]
        mask = mask_ref[slot, a, pl.ds(mask_at + b, 1), :]
        for q in range(tokens // BLOCK):
            lanes = slice(q * BLOCK, (q + 1) * BLOCK)
            dist = jnp.abs(kr - qr[:, lanes]) + jnp.abs(kg - qg[:, lanes])
            far[edge, b * BLOCK : (b + 1) * BLOCK, lanes] = jnp.where(mask[:, lanes] > 0.5, dist, FAR)


def fused_kernel(
    heads,
    weight_scale,
    slopes_ref,
    q_ref,
    k_ref,
    v_ref,
    up_in,
    w_ref,
    pos_ref,
    pairs_ref,
    count_ref,
    dq_ref,
    dk_ref,
    dv_ref,
    wg_ref,
    kb_ref,
    vb_ref,
    qb_ref,
    gb_ref,
    up_ref,
    og_ref,
    att_ref,
    attc_ref,
    dqs_ref,
    dks_ref,
    dvs_ref,
    cm_ref,
    mask_ref,
    stats_ref,
    col_ref,
    wbuf_ref,
    far_ref,
    fark_ref,
    top_ref,
    total_ref,
    acc_ref,
    dka_ref,
    dva_ref,
    part_ref,
    pland_ref,
    wsum_ref,
    ysum_ref,
    zland_ref,
    load_sem,
    zs_sem,
    zr_sem,
    ts_sem,
    tr_sem,
    ys_sem,
    yr_sem,
    wsend_sem,
    wrecv_sem,
    gsend_sem,
    grecv_sem,
    ysem,
    zsend_sem,
    zrecv_sem,
):
    tokens, width = q_ref.shape
    size = width // heads
    hl = heads // 2
    hw = width // 2
    blocks = tokens // BLOCK
    scaling = 1.0 / math.sqrt(size)
    n = lax.axis_size("ctx")
    nf = lax.axis_size("fsdp")
    me = lax.axis_index("ctx")
    fs = lax.axis_index("fsdp")
    wrows = w_ref.shape[0]
    model = up_ref.shape[1]
    half = n // 2
    wide = wsum_ref.shape[3]
    mask_rows = mask_ref.shape[2]
    y = lax.rem(me, 2)
    ny = 1 - y
    chunk = lax.div(me, 2)
    partner = {"ctx": me + 1 - 2 * y}
    ways = ({"ctx": lax.rem(me + 2, n)}, {"ctx": lax.rem(me + n - 2, n)})
    twin = fs + 1 - 2 * lax.rem(fs, 2)
    facing = lax.rem(fs + 2, nf)
    corner = lax.rem(twin + 2, nf)
    across = [{"ctx": lax.rem(me + 2 * d, n)} for d in range(1, half)]
    own_rows = pl.ds(pl.multiple_of(y * tokens, BLOCK), tokens)
    other_rows = pl.ds(pl.multiple_of(ny * tokens, BLOCK), tokens)
    own_cols = pl.ds(pl.multiple_of(y * hw, BLOCK), hw)
    other_cols = pl.ds(pl.multiple_of(ny * hw, BLOCK), hw)

    def rows_of(a):
        return pl.ds(pl.multiple_of(a * tokens, BLOCK), tokens)

    def chunk_of(slot):
        return lax.rem(chunk + lax.rem(slot + 1, 3) - 1 + half, half)

    barrier = pltpu.get_barrier_semaphore()
    friends = [partner] + across + [{"fsdp": twin}, {"fsdp": facing}]
    for friend in friends:
        pl.semaphore_signal(barrier, inc=1, device_id=friend, device_id_type=MESH)
    loads = [
        pltpu.make_async_copy(src, dst, load_sem.at[i])
        for i, (src, dst) in enumerate(
            (
                (k_ref.at[:, own_cols], kb_ref.at[0, own_rows, :]),
                (q_ref.at[:, own_cols], qb_ref.at[0, own_rows, :]),
                (v_ref.at[:, own_cols], vb_ref.at[0, own_rows, :]),
                (w_ref, wbuf_ref.at[3]),
                (up_in, up_ref),
            )
        )
    ]
    for load in loads:
        load.start()
    pl.semaphore_wait(barrier, len(friends))

    own_src = (k_ref, v_ref, q_ref, og_ref)
    chunk_buf = (kb_ref, vb_ref, qb_ref, gb_ref)

    def along(piece, part, way):
        which = min(piece, 3)
        buf = chunk_buf[which]
        rows = (own_rows, other_rows)[part]
        if piece < 3:
            cols, own = pl.ds(0, hw), own_cols
        else:
            h = piece - 3
            cols = pl.ds(h * size, size)
            own = pl.ds(pl.multiple_of(y * hw + h * size, BLOCK), size)
        src = own_src[which].at[:, own] if part == 0 else buf.at[0, rows, cols]
        return remote(src, buf.at[2 - way, rows, cols], zs_sem.at[piece, part, way], zr_sem.at[piece, part, way], ways[way])

    def start_along(piece, part):
        for way in (0, 1):
            along(piece, part, way).start()

    def landed(piece, part):
        for way in (0, 1):
            along(piece, part, way).wait_recv()

    def small(kind, way):
        if kind == 0:
            src, dst = stats_ref.at[0], stats_ref.at[2 - way]
        else:
            rows = pl.ds((1 - way) * mask_rows // 2, mask_rows // 2)
            src, dst = cm_ref.at[0, :, rows, :], cm_ref.at[2 - way, :, rows, :]
        return remote(src, dst, ts_sem.at[kind, way], tr_sem.at[kind, way], ways[way])

    def over(piece, mine=True):
        if piece < 4:
            src = own_src[piece].at[:, other_cols]
            dst = chunk_buf[piece].at[0, own_rows if mine else other_rows, :]
        elif piece == 4:
            src = cm_ref.at[0, y]
            dst = cm_ref.at[0, y if mine else ny]
        elif piece == 5:
            src = attc_ref.at[other_rows, :]
            dst = att_ref.at[:, own_cols if mine else other_cols]
        elif piece == 6:
            src = dqs_ref
            dst = dq_ref.at[:, own_cols if mine else other_cols]
        else:
            h = (piece - 7) // 2
            stage, out = ((dks_ref, dk_ref), (dvs_ref, dv_ref))[(piece - 7) % 2]
            src = stage.at[:, pl.ds(h * size, size)]
            at = (y if mine else ny) * hw + h * size
            dst = out.at[:, pl.ds(pl.multiple_of(at, BLOCK), size)]
        return remote(src, dst, ys_sem.at[piece], yr_sem.at[piece], partner)

    def met(piece):
        over(piece, False).wait_recv()

    for piece in (0, 1):
        over(piece).start()
        start_along(piece, 0)
    wcopies = [
        remote(
            wbuf_ref.at[1] if d == 2 else w_ref,
            wbuf_ref.at[d],
            wsend_sem.at[d],
            wrecv_sem.at[d],
            {"fsdp": facing if d == 1 else twin},
        )
        for d in range(3)
    ]
    wcopies[1].start()
    wcopies[0].start()
    over(2).start()

    lane = lax.broadcasted_iota(jnp.int32, (1, pairs_ref.shape[1]), 1)
    listed = lane < count_ref[0:1, 0:1]
    slot_iota = lax.broadcasted_iota(jnp.int32, (mask_rows, pairs_ref.shape[1]), 0)
    lane_iota = lax.broadcasted_iota(jnp.int32, (mask_rows, BLOCK), 1)
    compact = jnp.zeros((mask_rows, BLOCK), F32)
    for q in range(blocks):
        picked = jnp.where(listed & (pairs_ref[0:1, :] == q), pairs_ref[1:2, :], -1)
        hit = jnp.where(slot_iota == picked, 1.0, 0.0).astype(F32)
        hit = jnp.max(hit, axis=1, keepdims=True)
        compact = jnp.where(lane_iota == q, hit, compact)
    cm_ref[0, y] = compact
    over(4).start()

    def expand(slot, a, first, rows):
        small_mask = cm_ref[slot, a, first : first + rows, :]
        for q in range(blocks):
            mask_ref[slot, a, first : first + rows, q * BLOCK : (q + 1) * BLOCK] = jnp.broadcast_to(
                small_mask[:, q : q + 1], (rows, BLOCK)
            )

    expand(0, y, 0, mask_rows)

    @pl.loop(0, 6)
    def _(i):
        slot = lax.div(i, 2)
        node = 2 * chunk_of(slot) + lax.rem(i, 2)
        place = pos_ref[0:1, rows_of(node)]
        for c, part in enumerate((jnp.right_shift(place, GRID_BITS), jnp.bitwise_and(place, GRID - 1))):
            wide_part = jnp.broadcast_to(part.astype(F32), (BLOCK, tokens))
            col_ref[c, rows_of(i), :] = wide_part.T

    top_ref[...] = jnp.full(top_ref.shape, -1e30, F32)
    total_ref[...] = jnp.zeros(total_ref.shape, F32)
    acc_ref[...] = jnp.zeros(acc_ref.shape, F32)
    dka_ref[...] = jnp.zeros(dka_ref.shape, F32)
    dva_ref[...] = jnp.zeros(dva_ref.shape, F32)

    def measure(far, edge, qs, a, ks, b):
        shift = 2 * ((lax.rem(ks + 1, 3) - 1) - (lax.rem(qs + 1, 3) - 1)) + b - a
        build_distance(
            far, edge, col_ref, pos_ref, mask_ref, 2 * ks + b, 2 * chunk_of(qs) + a,
            (shift + REACH) * blocks, qs, a, tokens,
        )

    def local_edge(e):
        if isinstance(e, int) and e == 0:
            return y, 0, y
        c2 = lax.div(e - 1, 2)
        c1 = e - 1 - 2 * c2
        return ny + c2 * (y - ny), 0, ny + c1 * (y - ny)

    def far_edge(e):
        phase = lax.div(e - 4, 3)
        j = e - 4 - 3 * phase
        t = y + phase * (ny - y)
        c2 = lax.div(j, 2)
        c1 = j - 2 * c2
        c0 = 1 - c1 - c2
        return c0 + c2 * t, c0 + 2 * c1 + c2 * (1 + t), t

    def look(e, edge):
        a, ks, b = edge
        measure(far_ref, e, 0, a, ks, b)
        ka, qa = rows_of(b), rows_of(a)

        @pl.loop(0, hl)
        def _(h):
            hs = head_span(h, size)
            i = a * hl + h
            s = nt(kb_ref[ks, ka, hs], qb_ref[0, qa, hs]) * scaling - slopes_ref[y * hl + h] * far_ref[e]
            old = top_ref[i]
            new = jnp.maximum(old, jnp.max(s, axis=0, keepdims=True))
            factor = jnp.exp(old - new)
            p = jnp.exp(s - new)
            top_ref[i] = new
            total_ref[i] = total_ref[i] * factor + jnp.sum(p, axis=0, keepdims=True)
            acc_ref[i] = acc_ref[i] * factor + tn(vb_ref[ks, ka, hs], p.astype(BF16))

    def project(block, owner):
        cols = pl.ds(pl.multiple_of(owner * wrows, BLOCK), wrows)
        og_ref[:, cols] = nt(up_ref[...], block[...]).astype(BF16)

    for load in loads:
        load.wait()
    look(0, local_edge(0))
    project(wbuf_ref.at[3], fs)
    for piece in (0, 1):
        met(piece)
        start_along(piece, 1)
    start_along(2, 0)
    met(4)
    expand(0, ny, 0, mask_rows)
    met(2)
    start_along(2, 1)

    @pl.loop(1, 4)
    def _(e):
        look(e, local_edge(e))

    wcopies[1].wait()
    wcopies[2].start()
    project(wbuf_ref.at[1], facing)
    wcopies[0].wait()
    project(wbuf_ref.at[0], twin)
    wcopies[2].wait()
    project(wbuf_ref.at[2], corner)
    over(3).start()
    gb_ref[0, own_rows, :] = og_ref[:, own_cols]

    for phase in (0, 1):
        landed(0, phase)
        landed(1, phase)

        @pl.loop(4 + 3 * phase, 7 + 3 * phase)
        def _(e):
            look(e, far_edge(e))

    met(3)

    @pl.loop(0, 2 * hl)
    def _(i):
        a = lax.div(i, hl)
        h = i - a * hl
        hs = head_span(h, size)
        rows = rows_of(a)
        total = total_ref[i]
        att = (acc_ref[i] / total).T.astype(BF16)
        attc_ref[rows, hs] = att
        stats_ref[0, pl.ds(a * 2 * hl + h, 1), :] = top_ref[i] + jnp.log(total)
        prod = gb_ref[0, rows, hs].astype(F32) * att.astype(F32)
        stats_ref[0, pl.ds(a * 2 * hl + hl + h, 1), :] = jnp.sum(prod.T, axis=0, keepdims=True)
        acc_ref[i] = jnp.zeros((size, tokens), F32)

    for kind in (0, 1):
        for way in (0, 1):
            small(kind, way).start()
    over(5).start()
    for h in range(hl):
        for part in (1, 0):
            start_along(3 + h, part)
    att_ref[:, own_cols] = attc_ref[own_rows, :]

    def part_of(owner):
        cols = pl.ds(pl.multiple_of(owner * wrows, BLOCK), wrows)
        return tn(att_ref[:, cols], up_ref[...])

    gcopies = [
        remote(
            part_ref.at[d],
            pland_ref.at[d],
            gsend_sem.at[d],
            grecv_sem.at[d],
            {"fsdp": facing if d == 2 else twin},
        )
        for d in range(3)
    ]

    def visit(far, e, qs, a, ks, b, h, to_query, to_key):
        hs = head_span(h, size)
        ka, qa = rows_of(b), rows_of(a)
        k, q, g = kb_ref[ks, ka, hs], qb_ref[qs, qa, hs], gb_ref[qs, qa, hs]
        s = nt(k, q) * scaling - slopes_ref[y * hl + h] * far[e]
        p = jnp.exp(s - stats_ref[qs, pl.ds(a * 2 * hl + h, 1), :])
        delta = stats_ref[qs, pl.ds(a * 2 * hl + hl + h, 1), :]
        ds = (p * (nt(vb_ref[ks, ka, hs], g) - delta)).astype(BF16)
        if to_query:
            i = a * hl + h
            acc_ref[i] = acc_ref[i] + tn(k, ds)
        if to_key:
            i = b * hl + h
            dka_ref[i] = dka_ref[i] + nn(ds, q)
            dva_ref[i] = dva_ref[i] + nn(p.astype(BF16), g)

    def local_visits(first, last):
        @pl.loop(first, last)
        def _(e):
            head = 1 - lax.div(e + 3, 4)
            a, ks, b = local_edge(e + head)
            a = a + head * (y - ny)
            b = b + head * (y - ny)

            @pl.loop(0, hl)
            def _(h):
                visit(far_ref, e, 0, a, ks, b, h, True, True)

    local_visits(0, 2)
    met(5)
    part_ref[1] = part_of(corner).astype(BF16)
    gcopies[1].start()
    local_visits(2, 3)
    gcopies[1].wait()
    part_ref[2] = (part_of(facing) + pland_ref[1].astype(F32)).astype(BF16)
    gcopies[2].start()
    part_ref[0] = part_of(twin).astype(BF16)
    gcopies[0].start()
    local_visits(3, 4)

    def query_edges(first, last):
        @pl.loop(first, last)
        def _(e):
            a, ks, b = far_edge(e)

            @pl.loop(0, hl)
            def _(h):
                visit(far_ref, e, 0, a, ks, b, h, True, False)

    query_edges(4, 10)

    @pl.loop(0, hl)
    def _(h):
        hs = head_span(h, size)
        dqs_ref[:, hs] = (acc_ref[ny * hl + h].T * scaling).astype(BF16)
        dq_ref[:, pl.ds(pl.multiple_of(y * hw + h * size, BLOCK), size)] = (
            acc_ref[y * hl + h].T * scaling
        ).astype(BF16)

    over(6).start()

    gcopies[0].wait()
    gcopies[2].wait()
    mine = part_of(fs) + pland_ref[0].astype(F32) + pland_ref[2].astype(F32)
    for c in range(n):
        at = c * (model // n) // wide * wide
        wsum_ref[c % 2, c // 2] = mine[:, at : at + wide].astype(BF16)
    ycopy = remote(wsum_ref.at[ny], ysum_ref, ysem.at[0], ysem.at[1], partner)
    ycopy.start()

    for kind in (0, 1):
        for way in (0, 1):
            small(kind, way).wait_recv()
    for slot in (1, 2):
        for a in (0, 1):
            expand(slot, a, (slot - 1) * mask_rows // 2, mask_rows // 2)

    def key_edge(e):
        part = lax.div(e, 3)
        t = y + part * (ny - y)
        j = e - 3 * part
        c2 = lax.div(j, 2)
        c1 = j - 2 * c2
        c0 = 1 - c1 - c2
        return c0 * (1 + t) + c1 + 2 * c2, t, 0, c0 * (1 - t) + (1 - c0) * t

    @pl.loop(0, 6)
    def _(e):
        measure(fark_ref, e, *key_edge(e))

    for part in (0, 1):
        landed(2, part)

    def to_key(h):
        def edges(first, last):
            @pl.loop(first, last)
            def _(e):
                visit(fark_ref, e, *key_edge(e), h, False, True)

        landed(3 + h, 1)
        edges(3, 6)
        landed(3 + h, 0)
        edges(0, 1)
        hs = pl.ds(h * size, size)
        out = pl.ds(pl.multiple_of(y * hw + h * size, BLOCK), size)
        dks_ref[:, hs] = (dka_ref[ny * hl + h] * scaling).astype(BF16)
        dvs_ref[:, hs] = dva_ref[ny * hl + h].astype(BF16)
        over(7 + 2 * h).start()
        over(8 + 2 * h).start()
        edges(1, 3)
        dk_ref[:, out] = (dka_ref[y * hl + h] * scaling).astype(BF16)
        dv_ref[:, out] = dva_ref[y * hl + h].astype(BF16)

    to_key(0)
    to_key(1)
    ycopy.wait()
    zcopies = []
    for d in range(half):
        k = lax.rem(chunk + d, half)
        pair_sum = wsum_ref[y, k].astype(F32) + ysum_ref[k].astype(F32)
        if d == 0:
            wg_ref[...] = pair_sum
            continue
        zland_ref[0, d - 1] = pair_sum.astype(BF16)
        copy = remote(
            zland_ref.at[0, d - 1], zland_ref.at[1, d - 1], zsend_sem.at[d - 1], zrecv_sem.at[d - 1], across[d - 1]
        )
        copy.start()
        zcopies.append(copy)

    for h in range(2, hl):
        to_key(h)

    total = wg_ref[...]
    for d in range(1, half):
        zcopies[d - 1].wait()
        total = total + zland_ref[1, d - 1].astype(F32)
    wg_ref[...] = total * weight_scale
    for piece in range(6, 7 + 2 * hl):
        met(piece)
    for piece in range(7 + 2 * hl):
        over(piece).wait_send()
    for piece in range(3 + hl):
        for part in (0, 1):
            for way in (0, 1):
                along(piece, part, way).wait_send()
    for kind in (0, 1):
        for way in (0, 1):
            small(kind, way).wait_send()


def hand_over(*refs):
    sems = refs[8]
    copies = []
    for i in range(4):
        rows = refs[i].shape[0] // SPLIT
        for j in range(SPLIT):
            span = pl.ds(j * rows, rows)
            copies.append(pltpu.make_async_copy(refs[i].at[span], refs[4 + i].at[span], sems.at[i, j]))
    for copy in copies:
        copy.start()
    for copy in copies:
        copy.wait()


def on_device(
    queries, keys, values, upstream, out_weight, slopes, patch_index, pair_lists, pair_counts
):
    n = lax.axis_size("ctx")
    nf = lax.axis_size("fsdp")
    me = lax.axis_index("ctx")
    tokens, width = queries.shape[1:]
    model = upstream.shape[2]
    heads = slopes.shape[0]
    size = width // heads
    blocks = tokens // BLOCK
    window = 2 * REACH + 1
    slots = window * blocks
    mask_rows = -(-slots // 8) * 8

    vmem = pl.BlockSpec(memory_space=pltpu.VMEM)
    whole = pl.BlockSpec(memory_space=pl.ANY)
    smem = pl.BlockSpec(memory_space=pltpu.SMEM)
    block = jax.ShapeDtypeStruct((tokens, width), BF16)
    pair_flops = 2 * tokens * tokens * window * width
    wrows = out_weight.shape[0]
    cut = model // n
    wide = max(cut, BLOCK)
    half = n // 2
    hl = heads // 2
    hw = width // 2
    chunks = pltpu.VMEM((3, 2 * tokens, hw), BF16)
    stage = pltpu.VMEM((tokens, hw), BF16)
    dq, dk, dv, weight_grad = pl.pallas_call(
        functools.partial(fused_kernel, heads, 1.0 / math.sqrt(tokens * n * nf)),
        out_shape=(pltpu.VMEM((tokens, width), BF16),) * 3 + (pltpu.VMEM((wrows, wide), F32),),
        in_specs=[smem] + [whole] * 5 + [vmem] * 3,
        out_specs=(vmem,) * 4,
        scratch_shapes=[
            chunks,
            chunks,
            chunks,
            chunks,
            pltpu.VMEM((tokens, model), BF16),
            pltpu.VMEM((tokens, width), BF16),
            pltpu.VMEM((tokens, width), BF16),
            pltpu.VMEM((2 * tokens, hw), BF16),
            stage,
            stage,
            stage,
            pltpu.VMEM((3, 2, mask_rows, BLOCK), F32),
            pltpu.VMEM((3, 2, mask_rows, tokens), F32),
            pltpu.VMEM((3, 4 * hl, tokens), F32),
            pltpu.VMEM((2, 6 * tokens, BLOCK), F32),
            pltpu.VMEM((4,) + out_weight.shape, BF16),
            pltpu.VMEM((10, tokens, tokens), F32),
            pltpu.VMEM((6, tokens, tokens), F32),
            pltpu.VMEM((2 * hl, 1, tokens), F32),
            pltpu.VMEM((2 * hl, 1, tokens), F32),
            pltpu.VMEM((2 * hl, size, tokens), F32),
            pltpu.VMEM((2 * hl, tokens, size), F32),
            pltpu.VMEM((2 * hl, tokens, size), F32),
            pltpu.VMEM((3, wrows, model), BF16),
            pltpu.VMEM((3, wrows, model), BF16),
            pltpu.VMEM((2, half, wrows, wide), BF16),
            pltpu.VMEM((half, wrows, wide), BF16),
            pltpu.VMEM((2, half - 1, wrows, wide), BF16),
            pltpu.SemaphoreType.DMA((5,)),
            pltpu.SemaphoreType.DMA((3 + hl, 2, 2)),
            pltpu.SemaphoreType.DMA((3 + hl, 2, 2)),
            pltpu.SemaphoreType.DMA((2, 2)),
            pltpu.SemaphoreType.DMA((2, 2)),
            pltpu.SemaphoreType.DMA((7 + 2 * hl,)),
            pltpu.SemaphoreType.DMA((7 + 2 * hl,)),
            pltpu.SemaphoreType.DMA((3,)),
            pltpu.SemaphoreType.DMA((3,)),
            pltpu.SemaphoreType.DMA((3,)),
            pltpu.SemaphoreType.DMA((3,)),
            pltpu.SemaphoreType.DMA((2,)),
            pltpu.SemaphoreType.DMA((half - 1,)),
            pltpu.SemaphoreType.DMA((half - 1,)),
        ],
        compiler_params=pltpu.CompilerParams(
            collective_id=0, has_side_effects=True, vmem_limit_bytes=58 * 2**20
        ),
        cost_estimate=pl.CostEstimate(
            flops=10 * pair_flops, bytes_accessed=400 * 2**20, transcendentals=0
        ),
        name="fused",
    )(slopes, queries[0], keys[0], values[0], upstream[0], out_weight, patch_index, pair_lists[0], pair_counts)
    dq, dk, dv, weight_grad = pl.pallas_call(
        hand_over,
        out_shape=(block, block, block, jax.ShapeDtypeStruct((wrows, wide), F32)),
        in_specs=[vmem] * 4,
        out_specs=(whole,) * 4,
        scratch_shapes=[pltpu.SemaphoreType.DMA((4, SPLIT))],
        name="hand_over",
    )(*(pltpu.with_memory_space_constraint(x, pltpu.VMEM) for x in (dq, dk, dv, weight_grad)))
    if wide > cut:
        weight_grad = lax.dynamic_slice_in_dim(weight_grad, me * cut % wide, cut, 1)
    return (dq[None], dk[None], dv[None], weight_grad)


def solution(mesh):
    in_specs = (
        P("fsdp", "ctx", None),
        P("fsdp", "ctx", None),
        P("fsdp", "ctx", None),
        P("fsdp", "ctx", None),
        P("fsdp", None),
        P(),
        P("fsdp", None),
        P("fsdp", None, "ctx"),
        P("fsdp", "ctx"),
    )
    out_specs = (
        P("fsdp", "ctx", None),
        P("fsdp", "ctx", None),
        P("fsdp", "ctx", None),
        P("fsdp", "ctx"),
    )
    return jax.shard_map(
        on_device, mesh=mesh, in_specs=in_specs, out_specs=out_specs, check_vma=False
    )
```

```python
import functools
import math

import jax
import jax.numpy as jnp
from jax import lax
from jax.experimental import pallas as pl
from jax.experimental.pallas import tpu as pltpu
from jax.sharding import PartitionSpec as P

BLOCK = 128
REACH = 2
GRID = 1024
GRID_BITS = 10
SPLIT = 1
FAR = 1e32
MESH = pl.DeviceIdType.MESH
F32 = jnp.float32
BF16 = jnp.bfloat16


def nt(a, b):
    return lax.dot_general(a, b, (((1,), (1,)), ((), ())), preferred_element_type=F32)


def nn(a, b):
    return lax.dot_general(a, b, (((1,), (0,)), ((), ())), preferred_element_type=F32)


def tn(a, b):
    return lax.dot_general(a, b, (((0,), (0,)), ((), ())), preferred_element_type=F32)


def remote(src, dst, send_sem, recv_sem, target):
    return pltpu.make_async_remote_copy(
        src_ref=src, dst_ref=dst, send_sem=send_sem, recv_sem=recv_sem, device_id=target, device_id_type=MESH
    )


def head_span(h, size):
    return pl.ds(pl.multiple_of(h * size, size), size)


def build_distance(far, edge, col_ref, pos_ref, mask_ref, key_row, query_row, mask_at, slot, a, tokens):
    at = pl.multiple_of(query_row * tokens, BLOCK)
    query = pos_ref[0:1, pl.ds(at, tokens)]
    qr = jnp.right_shift(query, GRID_BITS).astype(F32)
    qg = jnp.bitwise_and(query, GRID - 1).astype(F32)
    for b in range(tokens // BLOCK):
        rows = pl.ds(pl.multiple_of(key_row * tokens + b * BLOCK, BLOCK), BLOCK)
        kr = col_ref[0, rows, :]
        kg = col_ref[1, rows, :]
        mask = mask_ref[slot, a, pl.ds(mask_at + b, 1), :]
        for q in range(tokens // BLOCK):
            lanes = slice(q * BLOCK, (q + 1) * BLOCK)
            dist = jnp.abs(kr - qr[:, lanes]) + jnp.abs(kg - qg[:, lanes])
            far[edge, b * BLOCK : (b + 1) * BLOCK, lanes] = jnp.where(mask[:, lanes] > 0.5, dist, FAR)


def fused_kernel(
    heads,
    weight_scale,
    slopes_ref,
    q_ref,
    k_ref,
    v_ref,
    up_in,
    w_ref,
    pos_ref,
    pairs_ref,
    count_ref,
    dq_ref,
    dk_ref,
    dv_ref,
    wg_ref,
    kb_ref,
    vb_ref,
    qb_ref,
    gb_ref,
    up_ref,
    og_ref,
    att_ref,
    attc_ref,
    dqs_ref,
    dks_ref,
    dvs_ref,
    cm_ref,
    mask_ref,
    stats_ref,
    col_ref,
    wbuf_ref,
    far_ref,
    fark_ref,
    top_ref,
    total_ref,
    acc_ref,
    dka_ref,
    dva_ref,
    part_ref,
    pland_ref,
    wsum_ref,
    ysum_ref,
    zland_ref,
    load_sem,
    zs_sem,
    zr_sem,
    ts_sem,
    tr_sem,
    ys_sem,
    yr_sem,
    wsend_sem,
    wrecv_sem,
    gsend_sem,
    grecv_sem,
    ysem,
    zsend_sem,
    zrecv_sem,
):
    tokens, width = q_ref.shape
    size = width // heads
    hl = heads // 2
    hw = width // 2
    blocks = tokens // BLOCK
    scaling = 1.0 / math.sqrt(size)
    n = lax.axis_size("ctx")
    nf = lax.axis_size("fsdp")
    me = lax.axis_index("ctx")
    fs = lax.axis_index("fsdp")
    wrows = w_ref.shape[0]
    model = up_ref.shape[1]
    half = n // 2
    wide = wsum_ref.shape[3]
    mask_rows = mask_ref.shape[2]
    y = lax.rem(me, 2)
    ny = 1 - y
    chunk = lax.div(me, 2)
    partner = {"ctx": me + 1 - 2 * y}
    ways = ({"ctx": lax.rem(me + 2, n)}, {"ctx": lax.rem(me + n - 2, n)})
    twin = fs + 1 - 2 * lax.rem(fs, 2)
    facing = lax.rem(fs + 2, nf)
    corner = lax.rem(twin + 2, nf)
    across = [{"ctx": lax.rem(me + 2 * d, n)} for d in range(1, half)]
    own_rows = pl.ds(pl.multiple_of(y * tokens, BLOCK), tokens)
    other_rows = pl.ds(pl.multiple_of(ny * tokens, BLOCK), tokens)
    own_cols = pl.ds(pl.multiple_of(y * hw, BLOCK), hw)
    other_cols = pl.ds(pl.multiple_of(ny * hw, BLOCK), hw)

    def rows_of(a):
        return pl.ds(pl.multiple_of(a * tokens, BLOCK), tokens)

    def chunk_of(slot):
        return lax.rem(chunk + lax.rem(slot + 1, 3) - 1 + half, half)

    barrier = pltpu.get_barrier_semaphore()
    friends = [partner] + across + [{"fsdp": twin}, {"fsdp": facing}]
    for friend in friends:
        pl.semaphore_signal(barrier, inc=1, device_id=friend, device_id_type=MESH)
    loads = [
        pltpu.make_async_copy(src, dst, load_sem.at[i])
        for i, (src, dst) in enumerate(
            (
                (k_ref.at[:, own_cols], kb_ref.at[0, own_rows, :]),
                (q_ref.at[:, own_cols], qb_ref.at[0, own_rows, :]),
                (v_ref.at[:, own_cols], vb_ref.at[0, own_rows, :]),
                (w_ref, wbuf_ref.at[3]),
                (up_in, up_ref),
            )
        )
    ]
    for load in loads:
        load.start()
    pl.semaphore_wait(barrier, len(friends))

    own_src = (k_ref, v_ref, q_ref, og_ref)
    chunk_buf = (kb_ref, vb_ref, qb_ref, gb_ref)

    def along(piece, part, way):
        which = min(piece, 3)
        buf = chunk_buf[which]
        rows = (own_rows, other_rows)[part]
        if piece < 3:
            cols, own = pl.ds(0, hw), own_cols
        else:
            h = piece - 3
            cols = pl.ds(h * size, size)
            own = pl.ds(pl.multiple_of(y * hw + h * size, BLOCK), size)
        src = own_src[which].at[:, own] if part == 0 else buf.at[0, rows, cols]
        target = {"ctx": lax.rem(me + 2 - 4 * way + n, n)}
        return remote(src, buf.at[2 - way, rows, cols], zs_sem.at[piece, part, way], zr_sem.at[piece, part, way], target)

    def start_along(piece, part):
        for way in (0, 1):
            along(piece, part, way).start()

    def landed(piece, part):
        for way in (0, 1):
            along(piece, part, way).wait_recv()

    def small(kind, way):
        if kind == 0:
            src, dst = stats_ref.at[0], stats_ref.at[2 - way]
        else:
            rows = pl.ds((1 - way) * mask_rows // 2, mask_rows // 2)
            src, dst = cm_ref.at[0, :, rows, :], cm_ref.at[2 - way, :, rows, :]
        return remote(src, dst, ts_sem.at[kind, way], tr_sem.at[kind, way], ways[way])

    def over(piece, mine=True):
        if piece < 4:
            src = own_src[piece].at[:, other_cols]
            dst = chunk_buf[piece].at[0, own_rows if mine else other_rows, :]
        elif piece == 4:
            src = cm_ref.at[0, y]
            dst = cm_ref.at[0, y if mine else ny]
        elif piece == 5:
            src = attc_ref.at[other_rows, :]
            dst = att_ref.at[:, own_cols if mine else other_cols]
        else:
            h, which = (piece - 6) % hl, (piece - 6) // hl
            stage, out = ((dqs_ref, dq_ref), (dks_ref, dk_ref), (dvs_ref, dv_ref))[which]
            src = stage.at[:, pl.ds(h * size, size)]
            at = (y if mine else ny) * hw + h * size
            dst = out.at[:, pl.ds(pl.multiple_of(at, BLOCK), size)]
        return remote(src, dst, ys_sem.at[piece], yr_sem.at[piece], partner)

    def met(piece):
        over(piece, False).wait_recv()

    for piece in (0, 1):
        over(piece).start()
        start_along(piece, 0)
    wcopies = [
        remote(
            wbuf_ref.at[1] if d == 2 else w_ref,
            wbuf_ref.at[d],
            wsend_sem.at[d],
            wrecv_sem.at[d],
            {"fsdp": facing if d == 1 else twin},
        )
        for d in range(3)
    ]
    wcopies[1].start()
    wcopies[0].start()
    over(2).start()

    lane = lax.broadcasted_iota(jnp.int32, (1, pairs_ref.shape[1]), 1)
    listed = lane < count_ref[0:1, 0:1]
    slot_iota = lax.broadcasted_iota(jnp.int32, (mask_rows, pairs_ref.shape[1]), 0)
    lane_iota = lax.broadcasted_iota(jnp.int32, (mask_rows, BLOCK), 1)
    compact = jnp.zeros((mask_rows, BLOCK), F32)
    for q in range(blocks):
        picked = jnp.where(listed & (pairs_ref[0:1, :] == q), pairs_ref[1:2, :], -1)
        hit = jnp.where(slot_iota == picked, 1.0, 0.0).astype(F32)
        hit = jnp.max(hit, axis=1, keepdims=True)
        compact = jnp.where(lane_iota == q, hit, compact)
    cm_ref[0, y] = compact
    over(4).start()

    def expand(slot, a, first, rows):
        small_mask = cm_ref[slot, a, first : first + rows, :]
        for q in range(blocks):
            mask_ref[slot, a, first : first + rows, q * BLOCK : (q + 1) * BLOCK] = jnp.broadcast_to(
                small_mask[:, q : q + 1], (rows, BLOCK)
            )

    expand(0, y, 0, mask_rows)

    @pl.loop(0, 6)
    def _(i):
        slot = lax.div(i, 2)
        node = 2 * chunk_of(slot) + lax.rem(i, 2)
        place = pos_ref[0:1, rows_of(node)]
        for c, part in enumerate((jnp.right_shift(place, GRID_BITS), jnp.bitwise_and(place, GRID - 1))):
            wide_part = jnp.broadcast_to(part.astype(F32), (BLOCK, tokens))
            col_ref[c, rows_of(i), :] = wide_part.T

    top_ref[...] = jnp.full(top_ref.shape, -1e30, F32)
    total_ref[...] = jnp.zeros(total_ref.shape, F32)
    acc_ref[...] = jnp.zeros(acc_ref.shape, F32)
    dka_ref[...] = jnp.zeros(dka_ref.shape, F32)
    dva_ref[...] = jnp.zeros(dva_ref.shape, F32)

    def measure(far, edge, qs, a, ks, b):
        shift = 2 * ((lax.rem(ks + 1, 3) - 1) - (lax.rem(qs + 1, 3) - 1)) + b - a
        build_distance(
            far, edge, col_ref, pos_ref, mask_ref, 2 * ks + b, 2 * chunk_of(qs) + a,
            (shift + REACH) * blocks, qs, a, tokens,
        )

    def local_edge(e):
        if isinstance(e, int) and e == 0:
            return y, 0, y
        c2 = lax.div(e - 1, 2)
        c1 = e - 1 - 2 * c2
        return ny + c2 * (y - ny), 0, ny + c1 * (y - ny)

    def far_edge(e):
        phase = lax.div(e - 4, 3)
        j = e - 4 - 3 * phase
        t = y + phase * (ny - y)
        c2 = lax.div(j, 2)
        c1 = j - 2 * c2
        c0 = 1 - c1 - c2
        return c0 + c2 * t, c0 + 2 * c1 + c2 * (1 + t), t

    def look(e, edge):
        a, ks, b = edge
        measure(far_ref, e, 0, a, ks, b)
        ka, qa = rows_of(b), rows_of(a)

        @pl.loop(0, hl)
        def _(h):
            hs = head_span(h, size)
            i = a * hl + h
            s = nt(kb_ref[ks, ka, hs], qb_ref[0, qa, hs]) * scaling - slopes_ref[y * hl + h] * far_ref[e]
            old = top_ref[i]
            new = jnp.maximum(old, jnp.max(s, axis=0, keepdims=True))
            factor = jnp.exp(old - new)
            p = jnp.exp(s - new)
            top_ref[i] = new
            total_ref[i] = total_ref[i] * factor + jnp.sum(p, axis=0, keepdims=True)
            acc_ref[i] = acc_ref[i] * factor + tn(vb_ref[ks, ka, hs], p.astype(BF16))

    def project(block, owner):
        cols = pl.ds(pl.multiple_of(owner * wrows, BLOCK), wrows)
        og_ref[:, cols] = nt(up_ref[...], block[...]).astype(BF16)

    for load in loads:
        load.wait()
    look(0, local_edge(0))
    project(wbuf_ref.at[3], fs)
    for piece in (0, 1):
        met(piece)
        start_along(piece, 1)
    start_along(2, 0)
    met(4)
    expand(0, ny, 0, mask_rows)
    met(2)
    start_along(2, 1)

    @pl.loop(1, 4)
    def _(e):
        look(e, local_edge(e))

    wcopies[1].wait()
    wcopies[2].start()
    project(wbuf_ref.at[1], facing)
    wcopies[0].wait()
    project(wbuf_ref.at[0], twin)
    wcopies[2].wait()
    project(wbuf_ref.at[2], corner)
    over(3).start()
    gb_ref[0, own_rows, :] = og_ref[:, own_cols]

    for phase in (0, 1):
        landed(0, phase)
        landed(1, phase)

        @pl.loop(4 + 3 * phase, 7 + 3 * phase)
        def _(e):
            look(e, far_edge(e))

    met(3)

    @pl.loop(0, 2 * hl)
    def _(i):
        a = lax.div(i, hl)
        h = i - a * hl
        hs = head_span(h, size)
        rows = rows_of(a)
        total = total_ref[i]
        att = (acc_ref[i] / total).T.astype(BF16)
        attc_ref[rows, hs] = att
        stats_ref[0, pl.ds(a * 2 * hl + h, 1), :] = top_ref[i] + jnp.log(total)
        prod = gb_ref[0, rows, hs].astype(F32) * att.astype(F32)
        stats_ref[0, pl.ds(a * 2 * hl + hl + h, 1), :] = jnp.sum(prod.T, axis=0, keepdims=True)
        acc_ref[i] = jnp.zeros((size, tokens), F32)

    for kind in (0, 1):
        for way in (0, 1):
            small(kind, way).start()
    over(5).start()
    for h in range(hl):
        start_along(3 + h, 1)
        along(3 + h, 0, ny).start()
    for h in range(hl):
        along(3 + h, 0, y).start()

    att_ref[:, own_cols] = attc_ref[own_rows, :]

    def part_of(owner):
        cols = pl.ds(pl.multiple_of(owner * wrows, BLOCK), wrows)
        return tn(att_ref[:, cols], up_ref[...])

    sides = (pl.ds(0, model // 2), pl.ds(model // 2, model // 2))
    gcopies = [
        remote(
            part_ref.at[min(d, 2), :, cols],
            pland_ref.at[min(d, 2), :, cols],
            gsend_sem.at[d],
            grecv_sem.at[d],
            {"fsdp": facing if d >= 2 else twin},
        )
        for d, cols in enumerate((pl.ds(0, model), pl.ds(0, model)) + sides)
    ]

    def visit(far, e, qs, a, ks, b, h, to_query, to_key):
        hs = head_span(h, size)
        ka, qa = rows_of(b), rows_of(a)
        k, q, g = kb_ref[ks, ka, hs], qb_ref[qs, qa, hs], gb_ref[qs, qa, hs]
        s = nt(k, q) * scaling - slopes_ref[y * hl + h] * far[e]
        p = jnp.exp(s - stats_ref[qs, pl.ds(a * 2 * hl + h, 1), :])
        delta = stats_ref[qs, pl.ds(a * 2 * hl + hl + h, 1), :]
        ds = (p * (nt(vb_ref[ks, ka, hs], g) - delta)).astype(BF16)
        if to_query:
            i = a * hl + h
            acc_ref[i] = acc_ref[i] + tn(k, ds)
        if to_key:
            i = b * hl + h
            dka_ref[i] = dka_ref[i] + nn(ds, q)
            dva_ref[i] = dva_ref[i] + nn(p.astype(BF16), g)

    def local_visits(h):
        @pl.loop(0, 4)
        def _(e):
            head = 1 - lax.div(e + 3, 4)
            a, ks, b = local_edge(e + head)
            visit(far_ref, e, 0, a + head * (y - ny), ks, b + head * (y - ny), h, True, True)

    def query_visits(h):
        @pl.loop(4, 10)
        def _(e):
            a, ks, b = far_edge(e)
            visit(far_ref, e, 0, a, ks, b, h, True, False)

        hs = pl.ds(h * size, size)
        dqs_ref[:, hs] = (acc_ref[ny * hl + h].T * scaling).astype(BF16)
        over(6 + h).start()
        dq_ref[:, pl.ds(pl.multiple_of(y * hw + h * size, BLOCK), size)] = (
            acc_ref[y * hl + h].T * scaling
        ).astype(BF16)

    ycopies = []

    def fold(j):
        gcopies[2 + j].wait()
        cols = pl.ds(pl.multiple_of(fs * wrows, BLOCK), wrows)
        mine = tn(att_ref[:, cols], up_ref[:, sides[j]])
        mine = mine + pland_ref[0, :, sides[j]].astype(F32) + pland_ref[2, :, sides[j]].astype(F32)
        for c in range(j * half, (j + 1) * half):
            at = c * (model // n) // wide * wide - j * (model // 2)
            wsum_ref[c % 2, c // 2] = mine[:, at : at + wide].astype(BF16)
        span = pl.ds(j * (half // 2), half // 2)
        copy = remote(wsum_ref.at[ny, span], ysum_ref.at[span], ysem.at[0, j], ysem.at[1, j], partner)
        copy.start()
        ycopies.append(copy)

    for h in range(hl):
        local_visits(h)
        if h == 1:
            gcopies[1].wait()
            part_ref[2] = (part_of(facing) + pland_ref[1].astype(F32)).astype(BF16)
            gcopies[2].start()
            gcopies[3].start()
            part_ref[0] = part_of(twin).astype(BF16)
            gcopies[0].start()
        query_visits(h)
        if h == 0:
            met(5)
            part_ref[1] = part_of(corner).astype(BF16)
            gcopies[1].start()
        if h == hl - 2:
            gcopies[0].wait()
            fold(0)
    fold(1)

    for kind in (0, 1):
        for way in (0, 1):
            small(kind, way).wait_recv()
    for slot in (1, 2):
        for a in (0, 1):
            expand(slot, a, (slot - 1) * mask_rows // 2, mask_rows // 2)

    def key_edge(e):
        part = lax.div(e, 3)
        t = y + part * (ny - y)
        j = e - 3 * part
        c2 = lax.div(j, 2)
        c0 = 1 - c2 - (j - 2 * c2)
        return 1 + t + c2 * (1 - 2 * t), t, 0, c0 * (1 - t) + (1 - c0) * t

    @pl.loop(0, 6)
    def _(e):
        measure(fark_ref, e, *key_edge(e))

    for part in (0, 1):
        landed(2, part)

    def key_edges(h, first, last):
        @pl.loop(first, last)
        def _(e):
            visit(fark_ref, e, *key_edge(e), h, False, True)

    def to_key(h):
        landed(3 + h, 1)
        key_edges(h, 3, 6)
        along(3 + h, 0, ny).wait_recv()
        key_edges(h, 0, 1)
        hs = pl.ds(h * size, size)
        dks_ref[:, hs] = (dka_ref[ny * hl + h] * scaling).astype(BF16)
        dvs_ref[:, hs] = dva_ref[ny * hl + h].astype(BF16)
        over(6 + hl + h).start()
        over(6 + 2 * hl + h).start()
        key_edges(h, 1, 2)

    def to_own_key(h):
        along(3 + h, 0, y).wait_recv()
        key_edges(h, 2, 3)
        out = pl.ds(pl.multiple_of(y * hw + h * size, BLOCK), size)
        dk_ref[:, out] = (dka_ref[y * hl + h] * scaling).astype(BF16)
        dv_ref[:, out] = dva_ref[y * hl + h].astype(BF16)

    def pair_sum(k):
        return wsum_ref[y, k].astype(F32) + ysum_ref[k].astype(F32)

    for copy in ycopies:
        copy.wait()
    zcopies = []
    for d in range(half):
        k = lax.rem(chunk + d, half)
        if d == 0:
            wg_ref[...] = pair_sum(k)
            continue
        zland_ref[0, d - 1] = pair_sum(k).astype(BF16)
        copy = remote(
            zland_ref.at[0, d - 1], zland_ref.at[1, d - 1], zsend_sem.at[d - 1], zrecv_sem.at[d - 1], across[d - 1]
        )
        copy.start()
        zcopies.append(copy)
    for h in range(hl):
        to_key(h)

    for h in range(hl):
        to_own_key(h)

    total = wg_ref[...]
    for d in range(1, half):
        zcopies[d - 1].wait()
        total = total + zland_ref[1, d - 1].astype(F32)
    wg_ref[...] = total * weight_scale
    for piece in range(6, 6 + 3 * hl):
        met(piece)
    for piece in range(6 + 3 * hl):
        over(piece).wait_send()
    for piece in range(3 + hl):
        for part in (0, 1):
            for way in (0, 1):
                along(piece, part, way).wait_send()
    for kind in (0, 1):
        for way in (0, 1):
            small(kind, way).wait_send()


def hand_over(*refs):
    sems = refs[8]
    copies = []
    for i in range(4):
        rows = refs[i].shape[0] // SPLIT
        for j in range(SPLIT):
            span = pl.ds(j * rows, rows)
            copies.append(pltpu.make_async_copy(refs[i].at[span], refs[4 + i].at[span], sems.at[i, j]))
    for copy in copies:
        copy.start()
    for copy in copies:
        copy.wait()


def on_device(
    queries, keys, values, upstream, out_weight, slopes, patch_index, pair_lists, pair_counts
):
    n = lax.axis_size("ctx")
    nf = lax.axis_size("fsdp")
    me = lax.axis_index("ctx")
    tokens, width = queries.shape[1:]
    model = upstream.shape[2]
    heads = slopes.shape[0]
    size = width // heads
    blocks = tokens // BLOCK
    window = 2 * REACH + 1
    slots = window * blocks
    mask_rows = -(-slots // 8) * 8

    vmem = pl.BlockSpec(memory_space=pltpu.VMEM)
    whole = pl.BlockSpec(memory_space=pl.ANY)
    smem = pl.BlockSpec(memory_space=pltpu.SMEM)
    block = jax.ShapeDtypeStruct((tokens, width), BF16)
    pair_flops = 2 * tokens * tokens * window * width
    wrows = out_weight.shape[0]
    cut = model // n
    wide = max(cut, BLOCK)
    half = n // 2
    hl = heads // 2
    hw = width // 2
    chunks = pltpu.VMEM((3, 2 * tokens, hw), BF16)
    stage = pltpu.VMEM((tokens, hw), BF16)
    dq, dk, dv, weight_grad = pl.pallas_call(
        functools.partial(fused_kernel, heads, 1.0 / math.sqrt(tokens * n * nf)),
        out_shape=(pltpu.VMEM((tokens, width), BF16),) * 3 + (pltpu.VMEM((wrows, wide), F32),),
        in_specs=[smem] + [whole] * 5 + [vmem] * 3,
        out_specs=(vmem,) * 4,
        scratch_shapes=[
            chunks,
            chunks,
            chunks,
            chunks,
            pltpu.VMEM((tokens, model), BF16),
            pltpu.VMEM((tokens, width), BF16),
            pltpu.VMEM((tokens, width), BF16),
            pltpu.VMEM((2 * tokens, hw), BF16),
            stage,
            stage,
            stage,
            pltpu.VMEM((3, 2, mask_rows, BLOCK), F32),
            pltpu.VMEM((3, 2, mask_rows, tokens), F32),
            pltpu.VMEM((3, 4 * hl, tokens), F32),
            pltpu.VMEM((2, 6 * tokens, BLOCK), F32),
            pltpu.VMEM((4,) + out_weight.shape, BF16),
            pltpu.VMEM((10, tokens, tokens), F32),
            pltpu.VMEM((6, tokens, tokens), F32),
            pltpu.VMEM((2 * hl, 1, tokens), F32),
            pltpu.VMEM((2 * hl, 1, tokens), F32),
            pltpu.VMEM((2 * hl, size, tokens), F32),
            pltpu.VMEM((2 * hl, tokens, size), F32),
            pltpu.VMEM((2 * hl, tokens, size), F32),
            pltpu.VMEM((3, wrows, model), BF16),
            pltpu.VMEM((3, wrows, model), BF16),
            pltpu.VMEM((2, half, wrows, wide), BF16),
            pltpu.VMEM((half, wrows, wide), BF16),
            pltpu.VMEM((2, half - 1, wrows, wide), BF16),
            pltpu.SemaphoreType.DMA((5,)),
            pltpu.SemaphoreType.DMA((3 + hl, 2, 2)),
            pltpu.SemaphoreType.DMA((3 + hl, 2, 2)),
            pltpu.SemaphoreType.DMA((2, 2)),
            pltpu.SemaphoreType.DMA((2, 2)),
            pltpu.SemaphoreType.DMA((6 + 3 * hl,)),
            pltpu.SemaphoreType.DMA((6 + 3 * hl,)),
            pltpu.SemaphoreType.DMA((3,)),
            pltpu.SemaphoreType.DMA((3,)),
            pltpu.SemaphoreType.DMA((4,)),
            pltpu.SemaphoreType.DMA((4,)),
            pltpu.SemaphoreType.DMA((2, 2)),
            pltpu.SemaphoreType.DMA((half - 1,)),
            pltpu.SemaphoreType.DMA((half - 1,)),
        ],
        compiler_params=pltpu.CompilerParams(
            collective_id=0, has_side_effects=True, vmem_limit_bytes=58 * 2**20
        ),
        cost_estimate=pl.CostEstimate(
            flops=10 * pair_flops, bytes_accessed=400 * 2**20, transcendentals=0
        ),
        name="fused",
    )(slopes, queries[0], keys[0], values[0], upstream[0], out_weight, patch_index, pair_lists[0], pair_counts)
    dq, dk, dv, weight_grad = pl.pallas_call(
        hand_over,
        out_shape=(block, block, block, jax.ShapeDtypeStruct((wrows, wide), F32)),
        in_specs=[vmem] * 4,
        out_specs=(whole,) * 4,
        scratch_shapes=[pltpu.SemaphoreType.DMA((4, SPLIT))],
        name="hand_over",
    )(*(pltpu.with_memory_space_constraint(x, pltpu.VMEM) for x in (dq, dk, dv, weight_grad)))
    if wide > cut:
        weight_grad = lax.dynamic_slice_in_dim(weight_grad, me * cut % wide, cut, 1)
    return (dq[None], dk[None], dv[None], weight_grad)


def solution(mesh):
    in_specs = (
        P("fsdp", "ctx", None),
        P("fsdp", "ctx", None),
        P("fsdp", "ctx", None),
        P("fsdp", "ctx", None),
        P("fsdp", None),
        P(),
        P("fsdp", None),
        P("fsdp", None, "ctx"),
        P("fsdp", "ctx"),
    )
    out_specs = (
        P("fsdp", "ctx", None),
        P("fsdp", "ctx", None),
        P("fsdp", "ctx", None),
        P("fsdp", "ctx"),
    )
    return jax.shard_map(
        on_device, mesh=mesh, in_specs=in_specs, out_specs=out_specs, check_vma=False
    )
```

```python
import functools
import math

import jax
import jax.numpy as jnp
from jax import lax
from jax.experimental import pallas as pl
from jax.experimental.pallas import tpu as pltpu
from jax.sharding import PartitionSpec as P

BLOCK = 128
REACH = 2
GRID = 1024
GRID_BITS = 10
SPLIT = 1
FAR = 1e32
MESH = pl.DeviceIdType.MESH
F32 = jnp.float32
BF16 = jnp.bfloat16


def nt(a, b):
    return lax.dot_general(a, b, (((1,), (1,)), ((), ())), preferred_element_type=F32)


def nn(a, b):
    return lax.dot_general(a, b, (((1,), (0,)), ((), ())), preferred_element_type=F32)


def tn(a, b):
    return lax.dot_general(a, b, (((0,), (0,)), ((), ())), preferred_element_type=F32)


def remote(src, dst, send_sem, recv_sem, target):
    return pltpu.make_async_remote_copy(
        src_ref=src, dst_ref=dst, send_sem=send_sem, recv_sem=recv_sem, device_id=target, device_id_type=MESH
    )


def head_span(h, size):
    return pl.ds(pl.multiple_of(h * size, size), size)


def build_distance(far, edge, col_ref, pos_ref, mask_ref, key_row, query_row, mask_at, slot, a, tokens):
    at = pl.multiple_of(query_row * tokens, BLOCK)
    query = pos_ref[0:1, pl.ds(at, tokens)]
    qr = jnp.right_shift(query, GRID_BITS).astype(F32)
    qg = jnp.bitwise_and(query, GRID - 1).astype(F32)
    for b in range(tokens // BLOCK):
        rows = pl.ds(pl.multiple_of(key_row * tokens + b * BLOCK, BLOCK), BLOCK)
        kr = col_ref[0, rows, :]
        kg = col_ref[1, rows, :]
        mask = mask_ref[slot, a, pl.ds(mask_at + b, 1), :]
        for q in range(tokens // BLOCK):
            lanes = slice(q * BLOCK, (q + 1) * BLOCK)
            dist = jnp.abs(kr - qr[:, lanes]) + jnp.abs(kg - qg[:, lanes])
            far[edge, b * BLOCK : (b + 1) * BLOCK, lanes] = jnp.where(mask[:, lanes] > 0.5, dist, FAR)


def fused_kernel(
    heads,
    weight_scale,
    slopes_ref,
    q_ref,
    k_ref,
    v_ref,
    up_in,
    w_ref,
    pos_ref,
    pairs_ref,
    count_ref,
    dq_ref,
    dk_ref,
    dv_ref,
    wg_ref,
    kb_ref,
    vb_ref,
    qb_ref,
    gb_ref,
    up_ref,
    og_ref,
    att_ref,
    attc_ref,
    dqs_ref,
    dks_ref,
    dvs_ref,
    cm_ref,
    mask_ref,
    stats_ref,
    col_ref,
    wbuf_ref,
    far_ref,
    prob_ref,
    seen_ref,
    fark_ref,
    top_ref,
    total_ref,
    acc_ref,
    dka_ref,
    dva_ref,
    part_ref,
    pland_ref,
    wsum_ref,
    ysum_ref,
    zland_ref,
    load_sem,
    zs_sem,
    zr_sem,
    ts_sem,
    tr_sem,
    ys_sem,
    yr_sem,
    wsend_sem,
    wrecv_sem,
    gsend_sem,
    grecv_sem,
    ysem,
    zsend_sem,
    zrecv_sem,
):
    tokens, width = q_ref.shape
    size = width // heads
    hl = heads // 2
    hw = width // 2
    blocks = tokens // BLOCK
    scaling = 1.0 / math.sqrt(size)
    n = lax.axis_size("ctx")
    nf = lax.axis_size("fsdp")
    me = lax.axis_index("ctx")
    fs = lax.axis_index("fsdp")
    wrows = w_ref.shape[0]
    model = up_ref.shape[1]
    half = n // 2
    wide = wsum_ref.shape[3]
    mask_rows = mask_ref.shape[2]
    y = lax.rem(me, 2)
    ny = 1 - y
    chunk = lax.div(me, 2)
    partner = {"ctx": me + 1 - 2 * y}
    ways = ({"ctx": lax.rem(me + 2, n)}, {"ctx": lax.rem(me + n - 2, n)})
    twin = fs + 1 - 2 * lax.rem(fs, 2)
    facing = lax.rem(fs + 2, nf)
    corner = lax.rem(twin + 2, nf)
    across = [{"ctx": lax.rem(me + 2 * d, n)} for d in range(1, half)]
    own_rows = pl.ds(pl.multiple_of(y * tokens, BLOCK), tokens)
    other_rows = pl.ds(pl.multiple_of(ny * tokens, BLOCK), tokens)
    own_cols = pl.ds(pl.multiple_of(y * hw, BLOCK), hw)
    other_cols = pl.ds(pl.multiple_of(ny * hw, BLOCK), hw)

    def rows_of(a):
        return pl.ds(pl.multiple_of(a * tokens, BLOCK), tokens)

    def chunk_of(slot):
        return lax.rem(chunk + lax.rem(slot + 1, 3) - 1 + half, half)

    barrier = pltpu.get_barrier_semaphore()
    friends = [partner] + across + [{"fsdp": twin}, {"fsdp": facing}]
    for friend in friends:
        pl.semaphore_signal(barrier, inc=1, device_id=friend, device_id_type=MESH)
    loads = [
        pltpu.make_async_copy(src, dst, load_sem.at[i])
        for i, (src, dst) in enumerate(
            (
                (k_ref.at[:, own_cols], kb_ref.at[0, own_rows, :]),
                (q_ref.at[:, own_cols], qb_ref.at[0, own_rows, :]),
                (v_ref.at[:, own_cols], vb_ref.at[0, own_rows, :]),
                (w_ref, wbuf_ref.at[3]),
                (up_in, up_ref),
            )
        )
    ]
    for load in loads:
        load.start()
    pl.semaphore_wait(barrier, len(friends))

    own_src = (k_ref, v_ref, q_ref, og_ref)
    chunk_buf = (kb_ref, vb_ref, qb_ref, gb_ref)

    def along(piece, part, way):
        which = min(piece, 3)
        buf = chunk_buf[which]
        rows = (own_rows, other_rows)[part]
        if piece < 3:
            cols, own = pl.ds(0, hw), own_cols
        else:
            h = piece - 3
            cols = pl.ds(h * size, size)
            own = pl.ds(pl.multiple_of(y * hw + h * size, BLOCK), size)
        src = own_src[which].at[:, own] if part == 0 else buf.at[0, rows, cols]
        target = {"ctx": lax.rem(me + 2 - 4 * way + n, n)}
        return remote(src, buf.at[2 - way, rows, cols], zs_sem.at[piece, part, way], zr_sem.at[piece, part, way], target)

    def start_along(piece, part):
        for way in (0, 1):
            along(piece, part, way).start()

    def landed(piece, part):
        for way in (0, 1):
            along(piece, part, way).wait_recv()

    def small(kind, way):
        if kind == 0:
            src, dst = stats_ref.at[0], stats_ref.at[2 - way]
        else:
            rows = pl.ds((1 - way) * mask_rows // 2, mask_rows // 2)
            src, dst = cm_ref.at[0, :, rows, :], cm_ref.at[2 - way, :, rows, :]
        return remote(src, dst, ts_sem.at[kind, way], tr_sem.at[kind, way], ways[way])

    def over(piece, mine=True):
        if piece < 4:
            src = own_src[piece].at[:, other_cols]
            dst = chunk_buf[piece].at[0, own_rows if mine else other_rows, :]
        elif piece == 4:
            src = cm_ref.at[0, y]
            dst = cm_ref.at[0, y if mine else ny]
        elif piece == 5:
            src = attc_ref.at[other_rows, :]
            dst = att_ref.at[:, own_cols if mine else other_cols]
        else:
            h, which = (piece - 6) % hl, (piece - 6) // hl
            stage, out = ((dqs_ref, dq_ref), (dks_ref, dk_ref), (dvs_ref, dv_ref))[which]
            src = stage.at[:, pl.ds(h * size, size)]
            at = (y if mine else ny) * hw + h * size
            dst = out.at[:, pl.ds(pl.multiple_of(at, BLOCK), size)]
        return remote(src, dst, ys_sem.at[piece], yr_sem.at[piece], partner)

    def met(piece):
        over(piece, False).wait_recv()

    for piece in (0, 1):
        over(piece).start()
        start_along(piece, 0)
    wcopies = [
        remote(
            wbuf_ref.at[1] if d == 2 else w_ref,
            wbuf_ref.at[d],
            wsend_sem.at[d],
            wrecv_sem.at[d],
            {"fsdp": facing if d == 1 else twin},
        )
        for d in range(3)
    ]
    wcopies[1].start()
    wcopies[0].start()
    over(2).start()

    lane = lax.broadcasted_iota(jnp.int32, (1, pairs_ref.shape[1]), 1)
    listed = lane < count_ref[0:1, 0:1]
    slot_iota = lax.broadcasted_iota(jnp.int32, (mask_rows, pairs_ref.shape[1]), 0)
    lane_iota = lax.broadcasted_iota(jnp.int32, (mask_rows, BLOCK), 1)
    compact = jnp.zeros((mask_rows, BLOCK), F32)
    for q in range(blocks):
        picked = jnp.where(listed & (pairs_ref[0:1, :] == q), pairs_ref[1:2, :], -1)
        hit = jnp.where(slot_iota == picked, 1.0, 0.0).astype(F32)
        hit = jnp.max(hit, axis=1, keepdims=True)
        compact = jnp.where(lane_iota == q, hit, compact)
    cm_ref[0, y] = compact
    over(4).start()

    def expand(slot, a, first, rows):
        small_mask = cm_ref[slot, a, first : first + rows, :]
        for q in range(blocks):
            mask_ref[slot, a, first : first + rows, q * BLOCK : (q + 1) * BLOCK] = jnp.broadcast_to(
                small_mask[:, q : q + 1], (rows, BLOCK)
            )

    expand(0, y, 0, mask_rows)

    @pl.loop(0, 6)
    def _(i):
        slot = lax.div(i, 2)
        node = 2 * chunk_of(slot) + lax.rem(i, 2)
        place = pos_ref[0:1, rows_of(node)]
        for c, part in enumerate((jnp.right_shift(place, GRID_BITS), jnp.bitwise_and(place, GRID - 1))):
            wide_part = jnp.broadcast_to(part.astype(F32), (BLOCK, tokens))
            col_ref[c, rows_of(i), :] = wide_part.T

    top_ref[...] = jnp.full(top_ref.shape, -1e30, F32)
    total_ref[...] = jnp.zeros(total_ref.shape, F32)
    acc_ref[...] = jnp.zeros(acc_ref.shape, F32)
    dka_ref[...] = jnp.zeros(dka_ref.shape, F32)
    dva_ref[...] = jnp.zeros(dva_ref.shape, F32)

    def measure(far, edge, qs, a, ks, b):
        shift = 2 * ((lax.rem(ks + 1, 3) - 1) - (lax.rem(qs + 1, 3) - 1)) + b - a
        build_distance(
            far, edge, col_ref, pos_ref, mask_ref, 2 * ks + b, 2 * chunk_of(qs) + a,
            (shift + REACH) * blocks, qs, a, tokens,
        )

    def local_edge(e):
        if isinstance(e, int) and e == 0:
            return y, 0, y
        c2 = lax.div(e - 1, 2)
        c1 = e - 1 - 2 * c2
        return ny + c2 * (y - ny), 0, ny + c1 * (y - ny)

    def far_edge(e):
        phase = lax.div(e - 4, 3)
        j = e - 4 - 3 * phase
        t = y + phase * (ny - y)
        c2 = lax.div(j, 2)
        c1 = j - 2 * c2
        c0 = 1 - c1 - c2
        return c0 + c2 * t, c0 + 2 * c1 + c2 * (1 + t), t

    def look(e, edge):
        a, ks, b = edge
        measure(far_ref, 0, 0, a, ks, b)
        ka, qa = rows_of(b), rows_of(a)

        @pl.loop(0, hl)
        def _(h):
            hs = head_span(h, size)
            i = a * hl + h
            s = nt(kb_ref[ks, ka, hs], qb_ref[0, qa, hs]) * scaling - slopes_ref[y * hl + h] * far_ref[0]
            old = top_ref[i]
            new = jnp.maximum(old, jnp.max(s, axis=0, keepdims=True))
            factor = jnp.exp(old - new)
            p = jnp.exp(s - new)
            rounded = p.astype(BF16)
            prob_ref[e * hl + h] = rounded
            seen_ref[e * hl + h] = new
            top_ref[i] = new
            total_ref[i] = total_ref[i] * factor + jnp.sum(p, axis=0, keepdims=True)
            acc_ref[i] = acc_ref[i] * factor + tn(vb_ref[ks, ka, hs], rounded)

    def project(block, owner):
        cols = pl.ds(pl.multiple_of(owner * wrows, BLOCK), wrows)
        og_ref[:, cols] = nt(up_ref[...], block[...]).astype(BF16)

    for load in loads:
        load.wait()
    look(0, local_edge(0))
    project(wbuf_ref.at[3], fs)
    for piece in (0, 1):
        met(piece)
        start_along(piece, 1)
    start_along(2, 0)
    met(4)
    expand(0, ny, 0, mask_rows)
    met(2)
    start_along(2, 1)

    @pl.loop(1, 4)
    def _(e):
        look(e, local_edge(e))

    wcopies[1].wait()
    wcopies[2].start()
    project(wbuf_ref.at[1], facing)
    wcopies[0].wait()
    project(wbuf_ref.at[0], twin)
    wcopies[2].wait()
    project(wbuf_ref.at[2], corner)
    over(3).start()
    gb_ref[0, own_rows, :] = og_ref[:, own_cols]

    for phase in (0, 1):
        landed(0, phase)
        landed(1, phase)

        @pl.loop(4 + 3 * phase, 7 + 3 * phase)
        def _(e):
            look(e, far_edge(e))

    met(3)

    @pl.loop(0, 2 * hl)
    def _(i):
        a = lax.div(i, hl)
        h = i - a * hl
        hs = head_span(h, size)
        rows = rows_of(a)
        total = total_ref[i]
        att = (acc_ref[i] / total).T.astype(BF16)
        attc_ref[rows, hs] = att
        stats_ref[0, pl.ds(a * 2 * hl + h, 1), :] = top_ref[i] + jnp.log(total)
        prod = gb_ref[0, rows, hs].astype(F32) * att.astype(F32)
        stats_ref[0, pl.ds(a * 2 * hl + hl + h, 1), :] = jnp.sum(prod.T, axis=0, keepdims=True)
        acc_ref[i] = jnp.zeros((size, tokens), F32)

    for kind in (0, 1):
        for way in (0, 1):
            small(kind, way).start()
    over(5).start()
    for h in range(hl):
        start_along(3 + h, 1)
        along(3 + h, 0, ny).start()
    for h in range(hl):
        along(3 + h, 0, y).start()

    att_ref[:, own_cols] = attc_ref[own_rows, :]

    def part_of(owner):
        cols = pl.ds(pl.multiple_of(owner * wrows, BLOCK), wrows)
        return tn(att_ref[:, cols], up_ref[...])

    sides = (pl.ds(0, model // 2), pl.ds(model // 2, model // 2))
    gcopies = [
        remote(
            part_ref.at[min(d, 2), :, cols],
            pland_ref.at[min(d, 2), :, cols],
            gsend_sem.at[d],
            grecv_sem.at[d],
            {"fsdp": facing if d >= 2 else twin},
        )
        for d, cols in enumerate((pl.ds(0, model), pl.ds(0, model)) + sides)
    ]

    def visit(far, e, qs, a, ks, b, h, to_query, to_key):
        hs = head_span(h, size)
        ka, qa = rows_of(b), rows_of(a)
        k, q, g = kb_ref[ks, ka, hs], qb_ref[qs, qa, hs], gb_ref[qs, qa, hs]
        top = stats_ref[qs, pl.ds(a * 2 * hl + h, 1), :]
        if to_query:
            p = prob_ref[e * hl + h].astype(F32) * jnp.exp(seen_ref[e * hl + h] - top)
        else:
            p = jnp.exp(nt(k, q) * scaling - slopes_ref[y * hl + h] * far[e] - top)
        delta = stats_ref[qs, pl.ds(a * 2 * hl + hl + h, 1), :]
        ds = (p * (nt(vb_ref[ks, ka, hs], g) - delta)).astype(BF16)
        if to_query:
            i = a * hl + h
            acc_ref[i] = acc_ref[i] + tn(k, ds)
        if to_key:
            i = b * hl + h
            dka_ref[i] = dka_ref[i] + nn(ds, q)
            dva_ref[i] = dva_ref[i] + nn(p.astype(BF16), g)

    def local_visits(h):
        @pl.loop(0, 4)
        def _(e):
            head = 1 - lax.div(e + 3, 4)
            a, ks, b = local_edge(e + head)
            visit(far_ref, e, 0, a + head * (y - ny), ks, b + head * (y - ny), h, True, True)

    def query_visits(h):
        @pl.loop(4, 10)
        def _(e):
            a, ks, b = far_edge(e)
            visit(far_ref, e, 0, a, ks, b, h, True, False)

        hs = pl.ds(h * size, size)
        dqs_ref[:, hs] = (acc_ref[ny * hl + h].T * scaling).astype(BF16)
        over(6 + h).start()
        dq_ref[:, pl.ds(pl.multiple_of(y * hw + h * size, BLOCK), size)] = (
            acc_ref[y * hl + h].T * scaling
        ).astype(BF16)

    ycopies = []

    def fold(j):
        gcopies[2 + j].wait()
        cols = pl.ds(pl.multiple_of(fs * wrows, BLOCK), wrows)
        mine = tn(att_ref[:, cols], up_ref[:, sides[j]])
        mine = mine + pland_ref[0, :, sides[j]].astype(F32) + pland_ref[2, :, sides[j]].astype(F32)
        for c in range(j * half, (j + 1) * half):
            at = c * (model // n) // wide * wide - j * (model // 2)
            wsum_ref[c % 2, c // 2] = mine[:, at : at + wide].astype(BF16)
        span = pl.ds(j * (half // 2), half // 2)
        copy = remote(wsum_ref.at[ny, span], ysum_ref.at[span], ysem.at[0, j], ysem.at[1, j], partner)
        copy.start()
        ycopies.append(copy)

    for h in range(hl):
        local_visits(h)
        if h == 1:
            gcopies[1].wait()
            part_ref[2] = (part_of(facing) + pland_ref[1].astype(F32)).astype(BF16)
            gcopies[2].start()
            gcopies[3].start()
            part_ref[0] = part_of(twin).astype(BF16)
            gcopies[0].start()
        query_visits(h)
        if h == 0:
            met(5)
            part_ref[1] = part_of(corner).astype(BF16)
            gcopies[1].start()
        if h == hl - 2:
            gcopies[0].wait()
            fold(0)
    fold(1)

    for kind in (0, 1):
        for way in (0, 1):
            small(kind, way).wait_recv()
    for slot in (1, 2):
        for a in (0, 1):
            expand(slot, a, (slot - 1) * mask_rows // 2, mask_rows // 2)

    def key_edge(e):
        part = lax.div(e, 3)
        t = y + part * (ny - y)
        j = e - 3 * part
        c2 = lax.div(j, 2)
        c0 = 1 - c2 - (j - 2 * c2)
        return 1 + t + c2 * (1 - 2 * t), t, 0, c0 * (1 - t) + (1 - c0) * t

    @pl.loop(0, 6)
    def _(e):
        measure(fark_ref, e, *key_edge(e))

    for part in (0, 1):
        landed(2, part)

    def key_edges(h, first, last):
        @pl.loop(first, last)
        def _(e):
            visit(fark_ref, e, *key_edge(e), h, False, True)

    def to_key(h):
        landed(3 + h, 1)
        key_edges(h, 3, 6)
        along(3 + h, 0, ny).wait_recv()
        key_edges(h, 0, 1)
        hs = pl.ds(h * size, size)
        dks_ref[:, hs] = (dka_ref[ny * hl + h] * scaling).astype(BF16)
        dvs_ref[:, hs] = dva_ref[ny * hl + h].astype(BF16)
        over(6 + hl + h).start()
        over(6 + 2 * hl + h).start()
        key_edges(h, 1, 2)

    def to_own_key(h):
        along(3 + h, 0, y).wait_recv()
        key_edges(h, 2, 3)
        out = pl.ds(pl.multiple_of(y * hw + h * size, BLOCK), size)
        dk_ref[:, out] = (dka_ref[y * hl + h] * scaling).astype(BF16)
        dv_ref[:, out] = dva_ref[y * hl + h].astype(BF16)

    def pair_sum(k):
        return wsum_ref[y, k].astype(F32) + ysum_ref[k].astype(F32)

    for copy in ycopies:
        copy.wait()
    zcopies = {}
    pairs = half // 2
    far_first = [0, pairs] + [d for d in range(1, half) if d != pairs]
    for d in far_first:
        k = lax.rem(chunk + d, half)
        if d == 0:
            wg_ref[...] = pair_sum(k)
            continue
        zland_ref[0, d - 1] = pair_sum(k).astype(BF16)
        copy = remote(
            zland_ref.at[0, d - 1], zland_ref.at[1, d - 1], zsend_sem.at[d - 1], zrecv_sem.at[d - 1], across[d - 1]
        )
        copy.start()
        zcopies[d] = copy
    for h in range(hl):
        to_key(h)

    for h in range(hl):
        to_own_key(h)

    total = wg_ref[...]
    for d in far_first[1:]:
        zcopies[d].wait()
        total = total + zland_ref[1, d - 1].astype(F32)
    wg_ref[...] = total * weight_scale
    for piece in range(6, 6 + 3 * hl):
        met(piece)
    for piece in range(6 + 3 * hl):
        over(piece).wait_send()
    for piece in range(3 + hl):
        for part in (0, 1):
            for way in (0, 1):
                along(piece, part, way).wait_send()
    for kind in (0, 1):
        for way in (0, 1):
            small(kind, way).wait_send()


def hand_over(*refs):
    sems = refs[8]
    copies = []
    for i in range(4):
        rows = refs[i].shape[0] // SPLIT
        for j in range(SPLIT):
            span = pl.ds(j * rows, rows)
            copies.append(pltpu.make_async_copy(refs[i].at[span], refs[4 + i].at[span], sems.at[i, j]))
    for copy in copies:
        copy.start()
    for copy in copies:
        copy.wait()


def on_device(
    queries, keys, values, upstream, out_weight, slopes, patch_index, pair_lists, pair_counts
):
    n = lax.axis_size("ctx")
    nf = lax.axis_size("fsdp")
    me = lax.axis_index("ctx")
    tokens, width = queries.shape[1:]
    model = upstream.shape[2]
    heads = slopes.shape[0]
    size = width // heads
    blocks = tokens // BLOCK
    window = 2 * REACH + 1
    slots = window * blocks
    mask_rows = -(-slots // 8) * 8

    vmem = pl.BlockSpec(memory_space=pltpu.VMEM)
    whole = pl.BlockSpec(memory_space=pl.ANY)
    smem = pl.BlockSpec(memory_space=pltpu.SMEM)
    block = jax.ShapeDtypeStruct((tokens, width), BF16)
    pair_flops = 2 * tokens * tokens * window * width
    wrows = out_weight.shape[0]
    cut = model // n
    wide = max(cut, BLOCK)
    half = n // 2
    hl = heads // 2
    hw = width // 2
    chunks = pltpu.VMEM((3, 2 * tokens, hw), BF16)
    stage = pltpu.VMEM((tokens, hw), BF16)
    dq, dk, dv, weight_grad = pl.pallas_call(
        functools.partial(fused_kernel, heads, 1.0 / math.sqrt(tokens * n * nf)),
        out_shape=(pltpu.VMEM((tokens, width), BF16),) * 3 + (pltpu.VMEM((wrows, wide), F32),),
        in_specs=[smem] + [whole] * 5 + [vmem] * 3,
        out_specs=(vmem,) * 4,
        scratch_shapes=[
            chunks,
            chunks,
            chunks,
            chunks,
            pltpu.VMEM((tokens, model), BF16),
            pltpu.VMEM((tokens, width), BF16),
            pltpu.VMEM((tokens, width), BF16),
            pltpu.VMEM((2 * tokens, hw), BF16),
            stage,
            stage,
            stage,
            pltpu.VMEM((3, 2, mask_rows, BLOCK), F32),
            pltpu.VMEM((3, 2, mask_rows, tokens), F32),
            pltpu.VMEM((3, 4 * hl, tokens), F32),
            pltpu.VMEM((2, 6 * tokens, BLOCK), F32),
            pltpu.VMEM((4,) + out_weight.shape, BF16),
            pltpu.VMEM((1, tokens, tokens), F32),
            pltpu.VMEM((10 * hl, tokens, tokens), BF16),
            pltpu.VMEM((10 * hl, 1, tokens), F32),
            pltpu.VMEM((6, tokens, tokens), F32),
            pltpu.VMEM((2 * hl, 1, tokens), F32),
            pltpu.VMEM((2 * hl, 1, tokens), F32),
            pltpu.VMEM((2 * hl, size, tokens), F32),
            pltpu.VMEM((2 * hl, tokens, size), F32),
            pltpu.VMEM((2 * hl, tokens, size), F32),
            pltpu.VMEM((3, wrows, model), BF16),
            pltpu.VMEM((3, wrows, model), BF16),
            pltpu.VMEM((2, half, wrows, wide), BF16),
            pltpu.VMEM((half, wrows, wide), BF16),
            pltpu.VMEM((2, half - 1, wrows, wide), BF16),
            pltpu.SemaphoreType.DMA((5,)),
            pltpu.SemaphoreType.DMA((3 + hl, 2, 2)),
            pltpu.SemaphoreType.DMA((3 + hl, 2, 2)),
            pltpu.SemaphoreType.DMA((2, 2)),
            pltpu.SemaphoreType.DMA((2, 2)),
            pltpu.SemaphoreType.DMA((6 + 3 * hl,)),
            pltpu.SemaphoreType.DMA((6 + 3 * hl,)),
            pltpu.SemaphoreType.DMA((3,)),
            pltpu.SemaphoreType.DMA((3,)),
            pltpu.SemaphoreType.DMA((4,)),
            pltpu.SemaphoreType.DMA((4,)),
            pltpu.SemaphoreType.DMA((2, 2)),
            pltpu.SemaphoreType.DMA((half - 1,)),
            pltpu.SemaphoreType.DMA((half - 1,)),
        ],
        compiler_params=pltpu.CompilerParams(
            collective_id=0, has_side_effects=True, vmem_limit_bytes=58 * 2**20
        ),
        cost_estimate=pl.CostEstimate(
            flops=10 * pair_flops, bytes_accessed=400 * 2**20, transcendentals=0
        ),
        name="fused",
    )(slopes, queries[0], keys[0], values[0], upstream[0], out_weight, patch_index, pair_lists[0], pair_counts)
    dq, dk, dv, weight_grad = pl.pallas_call(
        hand_over,
        out_shape=(block, block, block, jax.ShapeDtypeStruct((wrows, wide), F32)),
        in_specs=[vmem] * 4,
        out_specs=(whole,) * 4,
        scratch_shapes=[pltpu.SemaphoreType.DMA((4, SPLIT))],
        name="hand_over",
    )(*(pltpu.with_memory_space_constraint(x, pltpu.VMEM) for x in (dq, dk, dv, weight_grad)))
    if wide > cut:
        weight_grad = lax.dynamic_slice_in_dim(weight_grad, me * cut % wide, cut, 1)
    return (dq[None], dk[None], dv[None], weight_grad)


def solution(mesh):
    in_specs = (
        P("fsdp", "ctx", None),
        P("fsdp", "ctx", None),
        P("fsdp", "ctx", None),
        P("fsdp", "ctx", None),
        P("fsdp", None),
        P(),
        P("fsdp", None),
        P("fsdp", None, "ctx"),
        P("fsdp", "ctx"),
    )
    out_specs = (
        P("fsdp", "ctx", None),
        P("fsdp", "ctx", None),
        P("fsdp", "ctx", None),
        P("fsdp", "ctx"),
    )
    return jax.shard_map(
        on_device, mesh=mesh, in_specs=in_specs, out_specs=out_specs, check_vma=False
    )
```
